512 devices in a mesh: replica: 64 (over y, z), tensor: 8 (over x, core).
Axes of the slice: x: 4, y: 8, z: 8, core: 2. Of those that a mesh axis runs over, the one named last changes fastest.
Arguments:
- hidden: bfloat16 [2048, 1536], P(('replica', 'tensor')), may hold values from -6 to 6
- attn_gain: float32 [1536], replicated, may hold values from 0.25 to 1.75
- w_query: bfloat16 [1536, 1536], P(None, 'tensor'), may hold values from -0.625 to 0.625
- w_keyvalue: bfloat16 [1536, 8, 128], P(None, 'tensor'), may hold values from -0.4375 to 0.4375
- w_output: bfloat16 [1536, 1536], P('tensor'), may hold values from -0.625 to 0.625
- cache: bfloat16 [4608, 128, 8, 128], P('replica', None, 'tensor')
- page_table: int32 [2048, 16], P('replica'), may hold values from -1 to 199, as said below
- ctx_len: int32 [2048], P('replica'), may hold values from 1 to 2048, as said below
- move_dest: int32 [2048], P('replica'), may hold values from 0 to 63, as said below
- ffn_gain: float32 [1536], replicated, may hold values from 0.25 to 1.75
- router: bfloat16 [1536, 40], replicated, may hold values from -0.15625 to 0.15625
- routes: int32 [2048, 8], P('replica'), may hold values from 0 to 39, all different within a row
- w_in: bfloat16 [1536, 2, 1024], P(None, None, 'tensor'), may hold values from -0.15625 to 0.15625
- w_down: bfloat16 [1024, 1536], P('tensor'), may hold values from -0.25 to 0.25
Outputs:
- attended: bfloat16 [2048, 1536], P(('replica', 'tensor'))
- experts_out: bfloat16 [2048, 1536], P(('replica', 'tensor'))
The draws below stay inside these ranges and needn't reach their ends.
Inputs may be any that keep to these rules, and one draw needn't show every extreme that they name: `move_dest`: replica r's 32 entries name where its pool rows 40 to 71 go, in order: 16 other replicas, 2 pages each, never r itself; one replica drawn from the seed receives pages from every other. `page_table`: row i holds request i's pages in order and -1 after its last page; each request has one page or more; every lent page is used by exactly one request of the replica it goes to, and no pool page twice. `ctx_len`: with n pages in its row, a request holds between (n - 1) * 128 + 1 and n * 128 cached tokens. `routes`: each row names 8 different experts.
All inputs are finite; a program needn't handle non-finite values.
Results may differ from the reference program's by a relative error of at most 0.02.
Values may be sent and summed in bfloat16 or wider, within the bound.
A program may use at most 64 MiB of HBM per device.

```python
import math
import jax
import jax.numpy as jnp
from jax import lax

D = 1536
QHEADS = 24
KVHEADS = 8
HEAD_DIM = 64
EXPERTS = 40
TOPK = 8
FF = 512
WINDOW_EXPERTS = 2
PAGE = 128
MAXPAGES = 16
CAP = 2
REQ_REP = 32
LOCAL_PAGES = 40
FANOUT = 16
OUTGOING = 32
POOL = 72
REQS = 2048


def overflow_plan(key):
    replicas = REQS // REQ_REP
    hottest = jax.random.randint(jax.random.fold_in(key, 11), (), 0, replicas)
    replica_ids = jnp.arange(replicas, dtype=jnp.int32)

    def one_source(sender):
        subkey = jax.random.fold_in(jax.random.fold_in(key, 12), sender)
        jitter = jax.random.randint(subkey, (replicas,), 0, 4096)
        scores = jitter * replicas + replica_ids + 1
        scores = jnp.where(replica_ids == hottest, 0, scores)
        scores = jnp.where(replica_ids == sender, 4097 * replicas + 1, scores)
        ranking = jnp.argsort(scores, stable=True)
        chosen = jnp.sort(ranking[:FANOUT])
        return jnp.repeat(chosen, CAP, total_repeat_length=FANOUT * CAP).astype(jnp.int32)
    return jax.vmap(one_source)(replica_ids)


def page_plan(key):
    replicas = REQS // REQ_REP
    layout = overflow_plan(key)
    out_slots = jnp.arange(OUTGOING, dtype=jnp.int32)
    earlier = (layout[:, None, :] == layout[:, :, None]) & (out_slots[None, None, :] < out_slots[None, :, None])
    order_rank = jnp.sum(earlier, axis=2).astype(jnp.int32)
    senders = jnp.arange(replicas, dtype=jnp.int32)[:, None]
    remote_value = (POOL + senders * CAP + order_rank).reshape(-1)
    remote_dest = layout.reshape(-1)
    candidates = replicas * OUTGOING + LOCAL_PAGES
    listing = jnp.concatenate([remote_value, jnp.arange(LOCAL_PAGES, dtype=jnp.int32)])

    def one_replica(replica):
        subkey = jax.random.fold_in(jax.random.fold_in(key, 13), replica)
        key_a, key_b, key_c, key_d = jax.random.split(subkey, 4)
        category = jnp.concatenate([jnp.where(remote_dest == replica, 0, 2).astype(jnp.int32), jnp.ones((LOCAL_PAGES,), jnp.int32)])
        jitter = jax.random.randint(key_a, (candidates,), 0, 4096)
        scores = category * 16777216 + jitter * 4096 + jnp.arange(candidates, dtype=jnp.int32)
        listed = listing[jnp.argsort(scores, stable=True)]
        available = LOCAL_PAGES + jnp.sum((remote_dest == replica).astype(jnp.int32))
        halving = jax.random.randint(key_b, (REQ_REP,), 0, 3)
        capacity = jnp.right_shift(jnp.full((REQ_REP,), MAXPAGES, jnp.int32), halving)
        shuffle = jax.random.permutation(key_c, REQ_REP)
        standing = jnp.argsort(shuffle)
        surplus = (capacity - 1)[shuffle]
        before = (jnp.cumsum(surplus) - surplus)[standing]
        slot_grid = jnp.arange(MAXPAGES, dtype=jnp.int32)[None, :]
        order_pos = jnp.where(slot_grid == 0, standing[:, None], REQ_REP + before[:, None] + slot_grid - 1)
        occupied = (slot_grid < capacity[:, None]) & (order_pos < available)
        slot_table = jnp.where(occupied, listed[jnp.clip(order_pos, 0, candidates - 1)], -1)
        page_count = jnp.sum(occupied.astype(jnp.int32), axis=1)
        last_fill = jax.random.randint(key_d, (REQ_REP,), 1, PAGE + 1)
        return (slot_table.astype(jnp.int32), ((page_count - 1) * PAGE + last_fill).astype(jnp.int32))
    tables, lengths = jax.vmap(one_replica)(jnp.arange(replicas, dtype=jnp.int32))
    return (tables.reshape(REQS, MAXPAGES), lengths.reshape(REQS))


def draw_move_dest(key, part):
    return overflow_plan(key).reshape(-1)


def draw_page_table(key, part):
    return page_plan(key)[0]


def draw_ctx_len(key, part):
    return page_plan(key)[1]


def draw_cache(key, part):
    replicas = REQS // REQ_REP
    array_shape = (replicas * POOL, PAGE, KVHEADS, 2 * HEAD_DIM)
    subkey = jax.random.fold_in(key, 14)
    key_a = jax.random.fold_in(subkey, 0)
    key_lane = jnp.arange(2 * HEAD_DIM) < HEAD_DIM
    spread = jnp.where(key_lane, 3.0, 1.0).astype(jnp.float32)
    normal_draw = jax.random.normal(key_a, array_shape, jnp.float32)
    return (normal_draw * spread).astype(jnp.bfloat16)


def levels(rng, extent, cuts, smallest, largest):
    def one(position, parts):
        steps = jax.random.uniform(jax.random.fold_in(jax.random.fold_in(rng, 6), position), (parts,), jnp.float32, smallest / len(cuts), largest / len(cuts))
        return jnp.repeat(jnp.exp(steps), extent[position] // parts).reshape((-1,) + (1,) * (len(extent) - position - 1))

    factor_of = one(*cuts[0])
    for cut in cuts[1:]:
        factor_of = factor_of * one(*cut)
    return factor_of


def picks_of(rng, rows, number_of, top, lift):
    sequence = jax.random.permutation(jax.random.fold_in(rng, 1), number_of)
    boost = sequence
    for power in range(3):
        boost = boost * boost // number_of
    boost = boost * lift // number_of
    lots = jax.random.randint(jax.random.fold_in(rng, 2), (rows, number_of), 0, 4096) + boost
    fixed_rows = jax.random.permutation(jax.random.fold_in(rng, 3), rows)[jnp.arange(number_of) % rows]
    lots = jnp.where(jnp.arange(rows)[:, None] == fixed_rows[None, :], 1 << 14, lots)
    priority = lots * number_of + jnp.arange(number_of)
    return lax.top_k(priority.astype(jnp.int32), top)[1].astype(jnp.int32)


def scatter_about(key, shape, scale, bound, cuts=(), kind=jnp.bfloat16):
    result = jax.random.normal(key, shape, jnp.float32) * scale
    if len(cuts) > 0:
        result = levels(key, shape, cuts, -0.22, 0.18) * result
    return jnp.clip(result, min=-bound, max=bound).astype(kind)


def setup_inputs(seed: int = 0) -> dict:
    seeds = jax.random.split(jax.random.key(seed), 15)
    hidden = scatter_about(seeds[0], (REQS, D), 1.0, 6.0, ((0, 512),))
    attn_gain = jnp.clip(1.0 + 0.15 * jax.random.normal(seeds[1], (D,), jnp.float32), 0.25, 1.75)
    w_query = scatter_about(seeds[2], (D, QHEADS * HEAD_DIM), (D // 16) ** -0.5, 0.625, ((1, 8),))
    w_keyvalue = scatter_about(seeds[3], (D, KVHEADS, 2 * HEAD_DIM), (D // 9) ** -0.5, 0.4375, ((1, 8),))
    w_output = scatter_about(seeds[4], (QHEADS * HEAD_DIM, D), (QHEADS * HEAD_DIM // 16) ** -0.5, 0.625, ((0, 8),))
    cache = draw_cache(jax.random.fold_in(seeds[14], 71), 0)
    page_table = draw_page_table(jax.random.fold_in(seeds[14], 71), 0)
    ctx_len = draw_ctx_len(jax.random.fold_in(seeds[14], 71), 0)
    move_dest = draw_move_dest(jax.random.fold_in(seeds[14], 71), 0)
    ffn_gain = jnp.clip(1.0 + 0.15 * jax.random.normal(seeds[9], (D,), jnp.float32), 0.25, 1.75)
    router = scatter_about(seeds[10], (D, EXPERTS), D ** -0.5, 0.15625)
    routes = picks_of(seeds[11], REQS, EXPERTS, TOPK, 1638)
    w_in = scatter_about(seeds[12], (D, 2, WINDOW_EXPERTS * FF), D ** -0.5, 0.15625, ((2, 8),))
    w_down = scatter_about(seeds[13], (WINDOW_EXPERTS * FF, D), FF ** -0.5, 0.25, ((0, 8),))
    return {"hidden": hidden, "attn_gain": attn_gain, "w_query": w_query, "w_keyvalue": w_keyvalue, "w_output": w_output, "cache": cache, "page_table": page_table, "ctx_len": ctx_len, "move_dest": move_dest, "ffn_gain": ffn_gain, "router": router, "routes": routes, "w_in": w_in, "w_down": w_down}


ATTN_SCALE = 0.015625
RESID_SCALE = 0.22
ROPE_BASE = 10000.0
EPSILON = 1e-06
NEG_FILL = -1e+30

def rms_norm(row_block, gain):
    values = row_block.astype(jnp.float32)
    factor = lax.rsqrt(lax.optimization_barrier(jnp.mean(values * values, axis=-1, keepdims=True)) + EPSILON)
    return (values * factor * gain.astype(jnp.float32)).astype(jnp.bfloat16)

def rotate(values, positions):
    lanes = values.shape[-1]
    halfway = lanes // 2
    indices = jnp.arange(halfway, dtype=jnp.float32)
    inverse = jnp.exp(indices * (-2.0 * math.log(ROPE_BASE) / lanes))
    angles = positions.astype(jnp.float32)[:, None] * inverse[None, :]
    cosine = jnp.concatenate([jnp.cos(angles), jnp.cos(angles)], axis=-1)[:, None, :]
    sine_rep = jnp.concatenate([jnp.sin(angles), jnp.sin(angles)], axis=-1)[:, None, :]
    turned = jnp.concatenate([-values[..., halfway:], values[..., :halfway]], axis=-1)
    return values * cosine + turned * sine_rep

def page_partials(queries, page_rows, spans):
    head_dim = queries.shape[-1]
    keys_part = page_rows[..., :head_dim].astype(jnp.float32)
    values_part = page_rows[..., head_dim:].astype(jnp.float32)
    scores = jnp.einsum('pkgh,ptkh->pkgt', queries.astype(jnp.float32), keys_part) * ATTN_SCALE
    in_range = (jnp.arange(page_rows.shape[1], dtype=jnp.int32)[None, :] < spans[:, None])[:, None, None, :]
    scores = jnp.where(in_range, scores, NEG_FILL)
    part_max = lax.optimization_barrier(jnp.max(scores, axis=-1))
    weights = jnp.where(in_range, jnp.exp(scores - part_max[..., None]), 0.0)
    part_sum = lax.optimization_barrier(jnp.sum(weights, axis=-1))
    rounded = lax.optimization_barrier(weights.astype(jnp.bfloat16)).astype(jnp.float32)
    part_out = jnp.einsum('pkgt,ptkh->pkgh', rounded, values_part)
    return (part_max, part_sum, part_out)

def inbox_sources(move_dest, replica):
    replicas = move_dest.shape[0] // OUTGOING
    layout = move_dest.reshape(replicas, OUTGOING)
    out_slots = jnp.arange(OUTGOING, dtype=jnp.int32)
    earlier = (layout[:, None, :] == layout[:, :, None]) & (out_slots[None, None, :] < out_slots[None, :, None])
    order_rank = lax.optimization_barrier(jnp.sum(earlier, axis=2)).astype(jnp.int32)
    senders = jnp.arange(replicas, dtype=jnp.int32)[:, None]
    target = senders * CAP + order_rank
    rows_global = senders * POOL + LOCAL_PAGES + out_slots[None, :]
    matches = (layout == replica)[None] & (target[None] == jnp.arange(replicas * CAP, dtype=jnp.int32)[:, None, None])
    return lax.optimization_barrier(jnp.sum(jnp.where(matches, rows_global[None], 0), axis=(1, 2))).astype(jnp.int32)

def one_replica(replica, row_block, slot_table, lengths, chosen_ids, cache, move_dest, attn_gain, w_query, w_keyvalue, w_output, ffn_gain, router, w_in, w_down):
    requests = row_block.shape[0]
    groups = QHEADS // KVHEADS
    normed = rms_norm(row_block, attn_gain)
    queries = jnp.dot(normed, w_query, preferred_element_type=jnp.float32).reshape(requests, QHEADS, HEAD_DIM)
    queries = rotate(queries, lengths).astype(jnp.bfloat16).reshape(requests, KVHEADS, groups, HEAD_DIM)
    projected = jnp.dot(normed, w_keyvalue.reshape(D, KVHEADS * 2 * HEAD_DIM), preferred_element_type=jnp.float32).reshape(requests, KVHEADS, 2 * HEAD_DIM)
    new_key = rotate(projected[..., :HEAD_DIM], lengths).astype(jnp.bfloat16)
    new_value = projected[..., HEAD_DIM:].astype(jnp.bfloat16)
    entries = slot_table.reshape(-1).astype(jnp.int32)
    positions = jnp.arange(entries.shape[0], dtype=jnp.int32)
    owners = positions // MAXPAGES
    slot_idx = positions % MAXPAGES
    spans = jnp.where(entries >= 0, jnp.clip(lengths[owners] - slot_idx * PAGE, 0, PAGE), 0).astype(jnp.int32)
    inbox_rows = inbox_sources(move_dest, replica)
    inbox_index = jnp.clip(entries - POOL, 0, inbox_rows.shape[0] - 1)
    page_source = jnp.where(entries < POOL, replica * POOL + entries, inbox_rows[inbox_index])
    page_source = jnp.where(entries >= 0, page_source, 0).astype(jnp.int32)
    part_max, part_sum, part_out = page_partials(queries[owners], cache[page_source], spans)
    part_max = part_max.reshape(requests, MAXPAGES, KVHEADS, groups)
    part_sum = part_sum.reshape(requests, MAXPAGES, KVHEADS, groups)
    part_out = part_out.reshape(requests, MAXPAGES, KVHEADS, groups, HEAD_DIM)
    new_score = jnp.einsum('rkgh,rkh->rkg', queries.astype(jnp.float32), new_key.astype(jnp.float32)) * ATTN_SCALE
    highest = jnp.maximum(new_score, lax.optimization_barrier(jnp.max(part_max, axis=1)))
    rescale = jnp.exp(part_max - highest[:, None])
    fresh_weight = jnp.exp(new_score - highest)
    denominator = lax.optimization_barrier(jnp.sum(rescale * part_sum, axis=1)) + fresh_weight
    numerator = lax.optimization_barrier(jnp.sum(rescale[..., None] * part_out, axis=1)) + fresh_weight[..., None] * new_value.astype(jnp.float32)[:, :, None, :]
    attention = (numerator / denominator[..., None]).astype(jnp.bfloat16).reshape(requests, QHEADS * HEAD_DIM)
    summed = jnp.dot(attention, w_output, preferred_element_type=jnp.float32)
    attended = (row_block.astype(jnp.float32) + RESID_SCALE * summed).astype(jnp.bfloat16)
    ffn_input = rms_norm(attended, ffn_gain)
    logits = jnp.dot(ffn_input, router, preferred_element_type=jnp.float32)
    gate_weights = jax.nn.softmax(jnp.take_along_axis(logits, chosen_ids, axis=1), axis=-1)
    unit_expert = jnp.arange(WINDOW_EXPERTS * FF, dtype=jnp.int32) // FF
    spread = lax.optimization_barrier(jnp.sum(jnp.where(chosen_ids[:, :, None] == unit_expert[None, None, :], gate_weights[:, :, None], 0.0), axis=1))
    lifted = jnp.dot(ffn_input, w_in.reshape(D, 2 * WINDOW_EXPERTS * FF), preferred_element_type=jnp.float32).reshape(requests, 2, WINDOW_EXPERTS * FF)
    active = (jax.nn.silu(lifted[:, 0]) * lifted[:, 1] * spread).astype(jnp.bfloat16)
    experts_out = jnp.dot(active, w_down, preferred_element_type=jnp.float32).astype(jnp.bfloat16)
    return (attended, experts_out)

def reference(hidden, attn_gain, w_query, w_keyvalue, w_output, cache, page_table, ctx_len, move_dest, ffn_gain, router, routes, w_in, w_down):
    replicas = hidden.shape[0] // REQ_REP

    def per_replica(pieces):
        replica, row_block, slot_table, lengths, chosen_ids = pieces
        return one_replica(replica, row_block, slot_table, lengths, chosen_ids, cache, move_dest, attn_gain, w_query, w_keyvalue, w_output, ffn_gain, router, w_in, w_down)
    attended, experts_out = lax.map(per_replica, (jnp.arange(replicas, dtype=jnp.int32), hidden.reshape(replicas, REQ_REP, D), page_table.reshape(replicas, REQ_REP, MAXPAGES), ctx_len.reshape(replicas, REQ_REP), routes.reshape(replicas, REQ_REP, TOPK)))
    return (attended.reshape(REQS, D), experts_out.reshape(REQS, D))
```

```python
import functools
import math

import jax
import jax.numpy as jnp
from jax import lax
from jax.experimental import pallas as pl
from jax.experimental.pallas import tpu as pltpu
from jax.sharding import PartitionSpec as P

HEAD_DIM = 64
EXPERTS = 40
FF = 512
CAP = 2
PAGE = 128
GROUPS = 3
ROWS = 8

ATTN_SCALE = 0.015625
RESID_SCALE = 0.22
ROPE_BASE = 10000.0
EPSILON = 1e-06
NEG_FILL = -1e30

BF = jnp.bfloat16
F32 = jnp.float32
I32 = jnp.int32
MESH = pl.DeviceIdType.MESH


def iota(shape, axis):
    return lax.broadcasted_iota(I32, shape, axis)


def mm(a, b):
    return lax.dot_general(a, b, (((1,), (0,)), ((), ())), preferred_element_type=F32)


def mm_t(a, b):
    return lax.dot_general(a, b, (((1,), (1,)), ((), ())), preferred_element_type=F32)


def roll4(v):
    return pltpu.roll(v, 4, 0)


def unfold(p0, p1, tensors):
    low = iota((8, p0.shape[1]), 0) < 4
    parts = []
    for a in range(tensors // 2):
        lo = p0[16 * a : 16 * a + 8] + roll4(p1[16 * a : 16 * a + 8])
        hi = roll4(p0[16 * a + 8 : 16 * a + 16]) + p1[16 * a + 8 : 16 * a + 16]
        parts.append(jnp.where(low, lo, hi))
    return jnp.concatenate(parts, axis=0)


def expand(v, tensors):
    low = iota((8, v.shape[1]), 0) < 4
    first, second = [], []
    for a in range(tensors // 2):
        piece = v[8 * a : 8 * a + 8]
        turned = roll4(piece)
        first.append(jnp.where(low, piece, 0.0))
        second.append(jnp.where(low, 0.0, turned))
        first.append(jnp.where(low, turned, 0.0))
        second.append(jnp.where(low, 0.0, piece))
    return jnp.concatenate(first, axis=0).astype(BF), jnp.concatenate(second, axis=0).astype(BF)


def page_rows(q_rows, pages):
    count = pages.shape[0]
    lane = iota((count * 8, 128), 1)
    span = jnp.where(lane < 64, pltpu.roll(q_rows, 64, 1), q_rows)
    query = jnp.where(lane < 64, q_rows, 0.0).reshape(count, 8, 128).astype(BF)
    scores = lax.dot_general(
        query, pages, (((2,), (2,)), ((0,), (0,))), preferred_element_type=F32
    ).reshape(count * 8, 128) * ATTN_SCALE
    in_range = lane.astype(F32) < span
    scores = jnp.where(in_range, scores, NEG_FILL)
    top = jnp.max(scores, axis=1, keepdims=True)
    weights = jnp.where(in_range, jnp.exp(scores - top), 0.0)
    total = jnp.sum(weights, axis=1, keepdims=True)
    out = lax.dot_general(
        weights.reshape(count, 8, 128).astype(BF),
        pages,
        (((2,), (1,)), ((0,), (0,))),
        preferred_element_type=F32,
    ).reshape(count * 8, 128)
    coarse = top.astype(BF).astype(F32)
    rows = jnp.where(
        lane < 16, coarse, jnp.where(lane < 32, top - coarse, jnp.where(lane < 64, total, out))
    )
    return rows.astype(BF)


def kernel(
    R, T, B, NL, LOCAL, POOL, OUT, UNITS,
    hid, again, wq, wkv, wo, cache, ptab, ctx, mdest, fgain, router, routes, win, wdown,
    att_o, exp_o,
    hid_v, again_v, wq_v, wkv_v, wo_v, cache_v, ptab_v, ctx_v, mdest_v, fgain_v, router_v,
    routes_v, win_v, wdown_v, win_f, wgu_v, fold_v, a1_v, qg_v, loc_v, att_v, exp_v,
    xg, msg, inq, ret_s, ret, rs_s, rs, fg, es_s, es,
    isem, osem, ready, ssem, rsem,
):
    r = lax.axis_index("replica")
    t = lax.axis_index("tensor")
    D = hid.shape[1]
    H = D // 2
    NZ = math.isqrt(R)
    y, z = r // NZ, lax.rem(r, NZ)
    NIN = R * ROWS
    NR = GROUPS * B

    loads = []

    def load(src, dst):
        copy = pltpu.make_async_copy(src, dst, isem.at[len(loads)])
        copy.start()
        loads.append(copy)
        return copy

    get_hid = load(hid, hid_v)
    get_again = load(again, again_v)
    get_ptab = load(ptab, ptab_v)
    get_ctx = load(ctx, ctx_v)
    get_mdest = load(mdest, mdest_v)
    get_wq = load(wq, wq_v.at[0 : GROUPS * HEAD_DIM])
    get_wkv = load(wkv, wkv_v)
    get_cache = load(cache, cache_v)
    get_win = load(win, win_v)
    get_wo = load(wo, wo_v.at[0 : GROUPS * HEAD_DIM])
    get_wdown = load(wdown, wdown_v)
    get_router = load(router, router_v.at[0:EXPERTS])
    get_routes = load(routes, routes_v)
    get_fgain = load(fgain, fgain_v)

    barrier = pltpu.get_barrier_semaphore()
    for k in range(1, T):
        pl.semaphore_signal(barrier, inc=1, device_id=(r, lax.rem(t + k, T)), device_id_type=MESH)
    for k in range(1, NZ):
        pl.semaphore_signal(
            barrier, inc=1, device_id=(lax.rem(y + k, NZ) * NZ + z, t), device_id_type=MESH
        )
        pl.semaphore_signal(
            barrier, inc=1, device_id=(y * NZ + lax.rem(z + k, NZ), t), device_id_type=MESH
        )

    low8 = iota((8, H), 0) < 4

    def normalise(folded, gain):
        squares = jnp.sum(folded * folded, axis=1, keepdims=True)
        mean = (squares + roll4(jnp.broadcast_to(squares, (8, 128)))[:, 0:1]) * (1.0 / D)
        return folded * lax.rsqrt(mean + EPSILON) * gain

    def fold_gain(ref):
        left = jnp.broadcast_to(ref[:, 0:H], (8, H))
        right = jnp.broadcast_to(ref[:, H:D], (8, H))
        return jnp.where(low8, left, right)

    get_hid.wait()
    get_again.wait()
    hidden = hid_v[...].astype(F32)
    fold_v[0:4, :] = hidden[:, 0:H]
    fold_v[4:8, :] = hidden[:, H:D]
    xg[t] = normalise(fold_v[...], fold_gain(again_v)).astype(BF)

    pl.semaphore_wait(barrier, (T - 1) + 2 * (NZ - 1))
    for k in range(1, NZ):
        pl.semaphore_signal(
            ready, inc=1, device_id=(y * NZ + lax.rem(z + k, NZ), t), device_id_type=MESH
        )

    def share(buf, phase):
        for k in range(1, T):
            pltpu.make_async_remote_copy(
                buf.at[t], buf.at[t], ssem.at[phase], rsem.at[phase],
                device_id=(r, lax.rem(t + k, T)), device_id_type=MESH,
            ).start()

    def scatter(src, dst, phase):
        for k in range(1, T):
            peer = lax.rem(t + k, T)
            pltpu.make_async_remote_copy(
                src.at[peer], dst.at[t], ssem.at[phase], rsem.at[phase],
                device_id=(r, peer), device_id_type=MESH,
            ).start()

    def exchange(src, dst, phase):
        def step(k, carry):
            peer = lax.rem(r + k, R)
            pltpu.make_async_remote_copy(
                src.at[peer], dst.at[r], ssem.at[phase], rsem.at[phase],
                device_id=(peer, t), device_id_type=MESH,
            ).start()
            return carry

        lax.fori_loop(1, R, step, 0)

    def arrived(buf, sems, phase):
        part = buf.at[0 : buf.shape[0] - 1]
        pltpu.make_async_copy(part, part, sems.at[phase]).wait()

    share(xg, 0)

    get_ptab.wait()
    get_ctx.wait()
    get_mdest.wait()
    table = ptab_v[...]
    slots = table.shape[0]
    ctx_row = ctx_v[...]
    spans = jnp.where(
        table >= 0, jnp.clip(ctx_row - iota((slots, B), 0) * PAGE, 0, PAGE), 0
    )
    tile = (iota((B, 4 * B), 0) == (iota((B, 4 * B), 1) & (B - 1))).astype(F32).astype(BF)
    table_w = mm(table.astype(F32).astype(BF), tile)
    spans_w = mm(spans.astype(F32).astype(BF), tile)
    CH = 64 if NL % 64 == 0 and NIN % 64 == 0 else 32

    def claims(base, page, head):
        found = jnp.zeros((CH, 4 * B), F32)
        pages = page.astype(F32)
        for k in range(slots):
            found = found + jnp.where(pages == table_w[k : k + 1, :], spans_w[k : k + 1, :], 0.0)
        group = iota((CH, 4 * B), 1) // B
        flag = jnp.where((group == head) & (found > 0.0), 1.0, 0.0)
        rows = jnp.where(group == GROUPS, found, flag)
        a1_v[pl.ds(base, CH), :] = jnp.where(head < GROUPS, rows, 0.0).astype(BF)

    def local_claims(c, carry):
        row = iota((CH, 4 * B), 0) + c * CH
        page = jnp.where(row < LOCAL * 8, row >> 3, -2)
        claims(pl.multiple_of(c * CH, CH), page, row & 7)
        return carry

    def inbox_claims(c, carry):
        row = iota((CH, 4 * B), 0) + c * CH
        claims(pl.multiple_of(NL + c * CH, CH), POOL + (row >> 2), row & 3)
        return carry

    lax.fori_loop(0, NL // CH, local_claims, 0)
    lax.fori_loop(0, NIN // CH, inbox_claims, 0)

    dest_row = mdest_v[...]
    dest_sq = jnp.broadcast_to(dest_row, (OUT, OUT))
    sub_sq, lane_sq = iota((OUT, OUT), 0), iota((OUT, OUT), 1)
    dest_col = jnp.sum(jnp.where(sub_sq == lane_sq, dest_sq, 0).astype(F32), axis=1, keepdims=True)
    dest_f = dest_sq.astype(F32)
    earlier = (dest_col == dest_f) & (sub_sq < lane_sq)
    rank = jnp.sum(jnp.where(earlier, 1.0, 0.0), axis=0, keepdims=True)
    slot_row = dest_f * CAP + rank
    slot_sq = slot_row[0:8, :]
    NQ = OUT * 8
    grow = (iota((OUT, NQ), 0) == (iota((OUT, NQ), 1) >> 3)).astype(F32).astype(BF)
    slot_lane = mm(slot_sq.astype(BF), grow)[0:1, :]
    pick = iota((NQ, OUT), 1) == (iota((NQ, OUT), 0) >> 3)
    slot_sub = jnp.sum(
        jnp.where(pick, jnp.broadcast_to(slot_row[0:1, :], (NQ, OUT)), 0.0), axis=1, keepdims=True
    )

    def fetch_map():
        row, lane = iota((NQ, NIN), 0), iota((NQ, NIN), 1)
        same = (lane >> 2).astype(F32) == slot_sub
        hit = same & ((row & 7) == (lane & 3)) & ((lane & 3) < GROUPS)
        return jnp.where(hit, 1.0, 0.0).astype(BF)

    def place_map():
        row, lane = iota((NIN, NQ), 0), iota((NIN, NQ), 1)
        same = (row >> 2).astype(F32) == slot_lane
        hit = same & ((lane & 7) == (row & 3)) & ((row & 3) < GROUPS)
        return jnp.where(hit, 1.0, 0.0).astype(BF)

    sq_b = iota((B, B), 0) == iota((B, B), 1)
    ctx_col = jnp.sum(
        jnp.where(sq_b, jnp.broadcast_to(ctx_row, (B, B)), 0).astype(F32), axis=1, keepdims=True
    )
    lane_b = iota((B, 128), 1)
    freq = (lane_b & 31).astype(F32)
    angle = ctx_col * jnp.exp(freq * (-2.0 * math.log(ROPE_BASE) / HEAD_DIM))
    cosine = jnp.cos(angle)
    sine = jnp.sin(angle)
    front = (lane_b & 63) < 32
    sine = jnp.where(front, -sine, sine)

    def rotate(v):
        turned = jnp.where(front, pltpu.roll(v, 96, 1), pltpu.roll(v, 32, 1))
        return (v * cosine + turned * sine).astype(BF).astype(F32)

    inq[r] = jnp.zeros((ROWS, 128), BF)
    ret[r] = jnp.zeros((ROWS, 128), BF)
    wq_v[GROUPS * HEAD_DIM :, :] = jnp.zeros((HEAD_DIM, D), BF)
    wo_v[GROUPS * HEAD_DIM :, :] = jnp.zeros((HEAD_DIM, D), BF)
    router_v[EXPERTS:, :] = jnp.zeros((128 - EXPERTS, D), BF)
    get_wq.wait()
    get_wkv.wait()

    arrived(xg, rsem, 0)
    normed = xg[...].astype(F32).reshape(T * 8, H).astype(BF)
    q_all = [mm_t(normed, wq_v[:, c * H : (c + 1) * H]) for c in range(2)]
    kv_all = [mm(normed, wkv_v[c * H : (c + 1) * H, :]) for c in range(2)]
    q01 = rotate(unfold(q_all[0][:, 0:128], q_all[1][:, 0:128], T))
    q2 = rotate(unfold(q_all[0][:, 128:256], q_all[1][:, 128:256], T))
    new_kv = unfold(kv_all[0], kv_all[1], T)
    head_lane = lane_b < 64
    heads = [
        jnp.where(head_lane, q01, 0.0),
        jnp.where(head_lane, pltpu.roll(q01, 64, 1), 0.0),
        jnp.where(head_lane, q2, 0.0),
    ]
    marker = jnp.where(head_lane, 0.0, 1.0)
    qg_v[...] = jnp.concatenate(heads + [marker], axis=0).astype(BF)

    msg[...] = mm(a1_v[NL:, :], qg_v[...]).reshape(R, ROWS, 128).astype(BF)
    pl.semaphore_wait(ready, NZ - 1)
    exchange(msg, inq, 1)

    get_cache.wait()
    loc_v[0 : LOCAL * 8, :] = page_rows(
        mm(a1_v[0 : LOCAL * 8, :], qg_v[...]), cache_v[0:LOCAL]
    )
    if NL > LOCAL * 8:
        loc_v[LOCAL * 8 :, :] = jnp.zeros((NL - LOCAL * 8, 128), BF)
    eye = (iota((4 * B, 4 * B), 0) == iota((4 * B, 4 * B), 1)).astype(F32).astype(BF)
    owned_loc = mm_t(eye, a1_v[0:NL, :])[0:NR] > 0.5
    owned_in = mm_t(eye, a1_v[NL:, :])[0:NR] > 0.5
    lane_sel = iota((NR, 128), 1)
    max_sel = jnp.where((lane_sel == 0) | (lane_sel == 16), 1.0, 0.0).astype(BF)
    new_key = rotate(new_kv)
    new_score = jnp.concatenate(
        [jnp.sum(h * new_key, axis=1, keepdims=True) for h in heads], axis=0
    ) * ATTN_SCALE
    fresh = jnp.where(head_lane, 1.0, new_kv.astype(BF).astype(F32))
    fresh = jnp.concatenate([fresh] * GROUPS, axis=0)
    loc = loc_v[...]
    score_loc = jnp.where(owned_loc, mm_t(max_sel, loc), NEG_FILL)
    top_loc = jnp.maximum(new_score, jnp.max(score_loc, axis=1, keepdims=True))
    sum_loc = mm(jnp.exp(score_loc - top_loc).astype(BF), loc)
    sum_loc = sum_loc + jnp.exp(new_score - top_loc) * fresh
    fetch = fetch_map()
    place = place_map()

    arrived(inq, rsem, 1)
    sent = inq[...].astype(F32).reshape(NIN, 128).astype(BF)
    lent = page_rows(mm(fetch, sent), cache_v[LOCAL:POOL])
    ret_s[...] = mm(place, lent).reshape(R, ROWS, 128).astype(BF)
    exchange(ret_s, ret, 2)

    get_win.wait()
    win_f[...] = win_v[...].astype(F32)
    wgu_v[:, 0:UNITS] = win_f[pl.ds(0, D, stride=2), :].astype(BF)
    wgu_v[:, UNITS:] = win_f[pl.ds(1, D, stride=2), :].astype(BF)
    get_wo.wait()
    get_wdown.wait()
    get_router.wait()
    get_routes.wait()
    get_fgain.wait()
    eye_b = sq_b.astype(F32).astype(BF)
    chosen = mm_t(eye_b, routes_v[...].astype(F32).astype(BF))
    expert = iota((B, 128), 1)
    expert_f = expert.astype(F32)
    picked = jnp.zeros((B, 128), F32)
    for k in range(routes.shape[0]):
        picked = jnp.where(expert_f == chosen[:, k : k + 1], 1.0, picked)
    mine = expert == (t * UNITS) // FF
    gain_f = fold_gain(fgain_v)
    residual = fold_v[...]

    arrived(ret, rsem, 2)
    back = ret[...].astype(F32).reshape(NIN, 128).astype(BF)
    score_in = jnp.where(owned_in, mm_t(max_sel, back), NEG_FILL)
    top = jnp.maximum(top_loc, jnp.max(score_in, axis=1, keepdims=True))
    merged = jnp.exp(top_loc - top) * sum_loc + mm(jnp.exp(score_in - top).astype(BF), back)
    attention = (merged / merged[:, 32:33]).astype(BF).astype(F32)
    att0, att1, att2 = (attention[g * B : (g + 1) * B] for g in range(GROUPS))
    left = jnp.where(head_lane, pltpu.roll(att0, 64, 1), att1)
    right = jnp.where(head_lane, pltpu.roll(att2, 64, 1), 0.0)
    left1, left2 = expand(left, T)
    right1, right2 = expand(right, T)
    rows1 = jnp.concatenate([left1, right1], axis=1)
    rows2 = jnp.concatenate([left2, right2], axis=1)
    partial = mm(rows1, wo_v[:, 0:H]) + mm(rows2, wo_v[:, H:D])
    partial = partial.reshape(T, 8, H).astype(BF)
    rs_s[...] = partial
    scatter(rs_s, rs, 3)
    rs[t] = rs_s[t]
    arrived(rs, rsem, 3)
    summed = jnp.sum(rs[...].astype(F32), axis=0)
    attended = (residual + RESID_SCALE * summed).astype(BF)
    attended_f = attended.astype(F32)
    fg[t] = normalise(attended_f, gain_f).astype(BF)
    share(fg, 4)
    att_v[:, 0:H] = attended_f[0:4].astype(BF)
    att_v[:, H:D] = attended_f[4:8].astype(BF)
    put_att = pltpu.make_async_copy(att_v, att_o, osem.at[0])
    put_att.start()

    arrived(fg, rsem, 4)
    ffn = fg[...].astype(F32).reshape(T * 8, H).astype(BF)
    up_all = [mm(ffn, wgu_v[c * H : (c + 1) * H, :]) for c in range(2)]
    log_all = [mm_t(ffn, router_v[:, c * H : (c + 1) * H]) for c in range(2)]
    gate = unfold(up_all[0][:, 0:UNITS], up_all[1][:, 0:UNITS], T)
    up = unfold(up_all[0][:, UNITS:], up_all[1][:, UNITS:], T)
    logits = jnp.where(picked > 0.0, unfold(log_all[0], log_all[1], T), NEG_FILL)
    chances = jnp.exp(logits - jnp.max(logits, axis=1, keepdims=True))
    chances = jnp.where(picked > 0.0, chances, 0.0)
    share_of = jnp.sum(jnp.where(mine, chances, 0.0), axis=1, keepdims=True) / jnp.sum(
        chances, axis=1, keepdims=True
    )
    active = gate * (1.0 / (1.0 + jnp.exp(-gate))) * up * share_of
    act1, act2 = expand(active, T)
    down = mm(act1, wdown_v[:, 0:H]) + mm(act2, wdown_v[:, H:D])
    es_s[...] = down.reshape(T, 8, H).astype(BF)
    scatter(es_s, es, 5)
    es[t] = es_s[t]
    arrived(es, rsem, 5)
    experts = jnp.sum(es[...].astype(F32), axis=0)
    exp_v[:, 0:H] = experts[0:4].astype(BF)
    exp_v[:, H:D] = experts[4:8].astype(BF)
    put_exp = pltpu.make_async_copy(exp_v, exp_o, osem.at[1])
    put_exp.start()
    for phase, buf in enumerate((xg, inq, ret, rs, fg, es)):
        arrived(buf, ssem, phase)
    put_att.wait()
    put_exp.wait()


def on_device(
    hidden,
    attn_gain,
    w_query,
    w_keyvalue,
    w_output,
    cache,
    page_table,
    ctx_len,
    move_dest,
    ffn_gain,
    router,
    routes,
    w_in,
    w_down,
):
    R = lax.axis_size("replica")
    T = lax.axis_size("tensor")
    D = hidden.shape[1]
    H = D // 2
    B = page_table.shape[0]
    POOL = cache.shape[0]
    OUT = move_dest.shape[0]
    LOCAL = POOL - OUT
    UNITS = w_down.shape[0]
    NL = -(-LOCAL * 8 // 128) * 128
    NIN = R * ROWS
    args = (
        hidden,
        attn_gain.reshape(1, D),
        w_query.T,
        w_keyvalue.reshape(D, 2 * HEAD_DIM),
        w_output,
        cache.reshape(POOL, PAGE, 2 * HEAD_DIM),
        page_table.T,
        ctx_len.reshape(1, B),
        move_dest.reshape(1, OUT),
        ffn_gain.reshape(1, D),
        router.T,
        routes.T,
        w_in.reshape(2 * D, UNITS),
        w_down,
    )
    vm = pltpu.VMEM
    landing = [vm(a.shape, a.dtype) for a in args]
    landing[2] = vm((256, D), BF)
    landing[4] = vm((256, D), BF)
    landing[10] = vm((128, D), BF)
    any_spec = pl.BlockSpec(memory_space=pl.ANY)
    group = vm((T, 8, H), BF)
    inbox = vm((R, ROWS, 128), BF)
    scratch = landing + [
        vm((2 * D, UNITS), F32),
        vm((D, 2 * UNITS), BF),
        vm((8, H), F32),
        vm((NL + NIN, 4 * B), BF),
        vm((4 * B, 128), BF),
        vm((NL, 128), BF),
        vm((4, D), BF),
        vm((4, D), BF),
        group,
        inbox,
        inbox,
        inbox,
        inbox,
        group,
        group,
        group,
        group,
        group,
        pltpu.SemaphoreType.DMA((len(args),)),
        pltpu.SemaphoreType.DMA((2,)),
        pltpu.SemaphoreType.REGULAR,
        pltpu.SemaphoreType.DMA((6,)),
        pltpu.SemaphoreType.DMA((6,)),
    ]
    shape = jax.ShapeDtypeStruct((4, D), BF)
    return pl.pallas_call(
        functools.partial(kernel, R, T, B, NL, LOCAL, POOL, OUT, UNITS),
        out_shape=(shape, shape),
        in_specs=[any_spec] * len(args),
        out_specs=(any_spec, any_spec),
        scratch_shapes=scratch,
        name="decode_step",
        compiler_params=pltpu.CompilerParams(
            collective_id=0, has_side_effects=True, vmem_limit_bytes=32 * 1024 * 1024
        ),
    )(*args)


def solution(mesh):
    placed = (
        P(("replica", "tensor"), None),
        P(),
        P(None, "tensor"),
        P(None, "tensor", None),
        P("tensor", None),
        P("replica", None, "tensor", None),
        P("replica", None),
        P("replica"),
        P("replica"),
        P(),
        P(),
        P("replica", None),
        P(None, None, "tensor"),
        P("tensor", None),
    )
    return jax.shard_map(
        on_device,
        mesh=mesh,
        in_specs=placed,
        out_specs=(P(("replica", "tensor"), None), P(("replica", "tensor"), None)),
        check_vma=False,
    )
```

```python
import functools
import math

import jax
import jax.numpy as jnp
from jax import lax
from jax.experimental import pallas as pl
from jax.experimental.pallas import tpu as pltpu
from jax.sharding import PartitionSpec as P

HEAD_DIM = 64
EXPERTS = 40
FF = 512
CAP = 2
PAGE = 128
GROUPS = 3
ROWS = 8

ATTN_SCALE = 0.015625
RESID_SCALE = 0.22
ROPE_BASE = 10000.0
EPSILON = 1e-06
NEG_FILL = -1e30

BF = jnp.bfloat16
F32 = jnp.float32
I32 = jnp.int32
MESH = pl.DeviceIdType.MESH


def iota(shape, axis):
    return lax.broadcasted_iota(I32, shape, axis)


def mm(a, b):
    return lax.dot_general(a, b, (((1,), (0,)), ((), ())), preferred_element_type=F32)


def mm_t(a, b):
    return lax.dot_general(a, b, (((1,), (1,)), ((), ())), preferred_element_type=F32)


def roll4(v):
    return pltpu.roll(v, 4, 0)


def unfold(p0, p1, tensors):
    low = iota((8, p0.shape[1]), 0) < 4
    parts = []
    for a in range(tensors // 2):
        lo = p0[16 * a : 16 * a + 8] + roll4(p1[16 * a : 16 * a + 8])
        hi = roll4(p0[16 * a + 8 : 16 * a + 16]) + p1[16 * a + 8 : 16 * a + 16]
        parts.append(jnp.where(low, lo, hi))
    return jnp.concatenate(parts, axis=0)


def expand(v, tensors):
    low = iota((8, v.shape[1]), 0) < 4
    first, second = [], []
    for a in range(tensors // 2):
        piece = v[8 * a : 8 * a + 8]
        turned = roll4(piece)
        first.append(jnp.where(low, piece, 0.0))
        second.append(jnp.where(low, 0.0, turned))
        first.append(jnp.where(low, turned, 0.0))
        second.append(jnp.where(low, 0.0, piece))
    return jnp.concatenate(first, axis=0).astype(BF), jnp.concatenate(second, axis=0).astype(BF)


def page_rows(q_rows, pages):
    count = pages.shape[0]
    lane = iota((count * 8, 128), 1)
    span = jnp.where(lane < 64, pltpu.roll(q_rows, 64, 1), q_rows)
    query = jnp.where(lane < 64, q_rows, 0.0).reshape(count, 8, 128).astype(BF)
    scores = lax.dot_general(
        query, pages, (((2,), (2,)), ((0,), (0,))), preferred_element_type=F32
    ).reshape(count * 8, 128) * ATTN_SCALE
    in_range = lane.astype(F32) < span
    scores = jnp.where(in_range, scores, NEG_FILL)
    top = jnp.max(scores, axis=1, keepdims=True)
    weights = jnp.where(in_range, jnp.exp(scores - top), 0.0)
    total = jnp.sum(weights, axis=1, keepdims=True)
    out = lax.dot_general(
        weights.reshape(count, 8, 128).astype(BF),
        pages,
        (((2,), (1,)), ((0,), (0,))),
        preferred_element_type=F32,
    ).reshape(count * 8, 128)
    coarse = top.astype(BF).astype(F32)
    rows = jnp.where(
        lane < 16, coarse, jnp.where(lane < 32, top - coarse, jnp.where(lane < 64, total, out))
    )
    return rows.astype(BF)


def kernel(
    R, T, B, NL, LOCAL, POOL, OUT, UNITS,
    hid, again, wq, wkv, wo, cache, ptab, ctx, mdest, fgain, router, routes, win, wdown,
    both_o,
    hid_v, again_v, wq_v, wkv_v, wo_v, cache_v, ptab_v, ctx_v, mdest_v, fgain_v, router_v,
    routes_v, win_v, wdown_v, win_f, wgu_v, fold_v, a1_v, qg_v, loc_v,
    xg, msg, inq, ret_s, ret, rs_s, rs, fg, es_s, es,
    isem, ready, ssem, rsem,
):
    r = lax.axis_index("replica")
    t = lax.axis_index("tensor")
    D = hid.shape[1]
    H = D // 2
    NZ = math.isqrt(R)
    y, z = r // NZ, lax.rem(r, NZ)
    NIN = R * ROWS
    NR = GROUPS * B

    barrier = pltpu.get_barrier_semaphore()
    for k in range(1, T):
        pl.semaphore_signal(barrier, inc=1, device_id=(r, lax.rem(t + k, T)), device_id_type=MESH)
    for k in range(1, NZ):
        pl.semaphore_signal(
            barrier, inc=1, device_id=(lax.rem(y + k, NZ) * NZ + z, t), device_id_type=MESH
        )
        pl.semaphore_signal(
            barrier, inc=1, device_id=(y * NZ + lax.rem(z + k, NZ), t), device_id_type=MESH
        )

    loads = []

    def load(src, dst):
        copy = pltpu.make_async_copy(src, dst, isem.at[len(loads)])
        copy.start()
        loads.append(copy)
        return copy

    get_hid = load(hid, hid_v)
    get_again = load(again, again_v)
    get_ptab = load(ptab, ptab_v)
    get_ctx = load(ctx, ctx_v)
    get_mdest = load(mdest, mdest_v)
    get_wq = load(wq, wq_v.at[0 : GROUPS * HEAD_DIM])
    get_wkv = load(wkv, wkv_v)
    get_cache = load(cache, cache_v)
    get_win = load(win, win_v)
    get_wo = load(wo, wo_v.at[0 : GROUPS * HEAD_DIM])
    get_wdown = load(wdown, wdown_v)
    get_router = load(router, router_v.at[0:EXPERTS])
    get_routes = load(routes, routes_v)
    get_fgain = load(fgain, fgain_v)

    low8 = iota((8, H), 0) < 4

    def normalise(folded, gain):
        squares = jnp.sum(folded * folded, axis=1, keepdims=True)
        mean = (squares + roll4(jnp.broadcast_to(squares, (8, 128)))[:, 0:1]) * (1.0 / D)
        return folded * lax.rsqrt(mean + EPSILON) * gain

    def fold_gain(ref):
        left = jnp.broadcast_to(ref[0:H].reshape(1, H), (8, H))
        right = jnp.broadcast_to(ref[H:D].reshape(1, H), (8, H))
        return jnp.where(low8, left, right)

    get_hid.wait()
    get_again.wait()
    hidden = hid_v[...].astype(F32)
    fold_v[0:4, :] = hidden[:, 0:H]
    fold_v[4:8, :] = hidden[:, H:D]
    xg[t] = normalise(fold_v[...], fold_gain(again_v)).astype(BF)

    pl.semaphore_wait(barrier, (T - 1) + 2 * (NZ - 1))
    for k in range(1, NZ):
        pl.semaphore_signal(
            ready, inc=1, device_id=(y * NZ + lax.rem(z + k, NZ), t), device_id_type=MESH
        )

    def share(buf, phase):
        for k in range(1, T):
            pltpu.make_async_remote_copy(
                buf.at[t], buf.at[t], ssem.at[phase], rsem.at[phase],
                device_id=(r, lax.rem(t + k, T)), device_id_type=MESH,
            ).start()

    def scatter(src, dst, phase):
        for k in range(1, T):
            peer = lax.rem(t + k, T)
            pltpu.make_async_remote_copy(
                src.at[peer], dst.at[t], ssem.at[phase], rsem.at[phase],
                device_id=(r, peer), device_id_type=MESH,
            ).start()

    offsets = sorted(
        ((dy, dz) for dy in range(NZ) for dz in range(NZ) if dy or dz),
        key=lambda d: -(min(d[0], NZ - d[0]) + min(d[1], NZ - d[1])),
    )

    def exchange(src, dst, phase):
        for dy, dz in offsets:
            peer = lax.rem(y + dy, NZ) * NZ + lax.rem(z + dz, NZ)
            pltpu.make_async_remote_copy(
                src.at[peer], dst.at[r], ssem.at[phase], rsem.at[phase],
                device_id=(peer, t), device_id_type=MESH,
            ).start()

    def arrived(buf, sems, phase):
        part = buf.at[0 : buf.shape[0] - 1]
        pltpu.make_async_copy(part, part, sems.at[phase]).wait()

    share(xg, 0)

    get_ptab.wait()
    get_ctx.wait()
    get_mdest.wait()
    table = ptab_v[...]
    slots = table.shape[0]
    ctx_row = ctx_v[...]
    spans = jnp.where(
        table >= 0, jnp.clip(ctx_row - iota((slots, B), 0) * PAGE, 0, PAGE), 0
    )
    tile = (iota((B, 4 * B), 0) == (iota((B, 4 * B), 1) & (B - 1))).astype(F32).astype(BF)
    table_w = mm(table.astype(F32).astype(BF), tile)
    spans_w = mm(spans.astype(F32).astype(BF), tile)
    CH = 64 if NL % 64 == 0 and NIN % 64 == 0 else 32

    def claims(base, page, head):
        found = jnp.zeros((CH, 4 * B), F32)
        pages = page.astype(F32)
        for k in range(slots):
            found = found + jnp.where(pages == table_w[k : k + 1, :], spans_w[k : k + 1, :], 0.0)
        group = iota((CH, 4 * B), 1) // B
        flag = jnp.where((group == head) & (found > 0.0), 1.0, 0.0)
        rows = jnp.where(group == GROUPS, found, flag)
        a1_v[pl.ds(base, CH), :] = jnp.where(head < GROUPS, rows, 0.0).astype(BF)

    def local_claims(c, carry):
        row = iota((CH, 4 * B), 0) + c * CH
        page = jnp.where(row < LOCAL * 8, row >> 3, -2)
        claims(pl.multiple_of(c * CH, CH), page, row & 7)
        return carry

    def inbox_claims(c, carry):
        row = iota((CH, 4 * B), 0) + c * CH
        claims(pl.multiple_of(NL + c * CH, CH), POOL + (row >> 2), row & 3)
        return carry

    lax.fori_loop(0, NL // CH, local_claims, 0)
    lax.fori_loop(0, NIN // CH, inbox_claims, 0)

    dest_row = mdest_v[...]
    dest_sq = jnp.broadcast_to(dest_row, (OUT, OUT))
    sub_sq, lane_sq = iota((OUT, OUT), 0), iota((OUT, OUT), 1)
    dest_col = jnp.sum(jnp.where(sub_sq == lane_sq, dest_sq, 0).astype(F32), axis=1, keepdims=True)
    dest_f = dest_sq.astype(F32)
    earlier = (dest_col == dest_f) & (sub_sq < lane_sq)
    rank = jnp.sum(jnp.where(earlier, 1.0, 0.0), axis=0, keepdims=True)
    slot_row = dest_f * CAP + rank
    slot_sq = slot_row[0:8, :]
    NQ = OUT * 8
    grow = (iota((OUT, NQ), 0) == (iota((OUT, NQ), 1) >> 3)).astype(F32).astype(BF)
    slot_lane = mm(slot_sq.astype(BF), grow)[0:1, :]
    pick = iota((NQ, OUT), 1) == (iota((NQ, OUT), 0) >> 3)
    slot_sub = jnp.sum(
        jnp.where(pick, jnp.broadcast_to(slot_row[0:1, :], (NQ, OUT)), 0.0), axis=1, keepdims=True
    )

    def fetch_map():
        row, lane = iota((NQ, NIN), 0), iota((NQ, NIN), 1)
        same = (lane >> 2).astype(F32) == slot_sub
        hit = same & ((row & 7) == (lane & 3)) & ((lane & 3) < GROUPS)
        return jnp.where(hit, 1.0, 0.0).astype(BF)

    def place_map():
        row, lane = iota((NIN, NQ), 0), iota((NIN, NQ), 1)
        same = (row >> 2).astype(F32) == slot_lane
        hit = same & ((lane & 7) == (row & 3)) & ((row & 3) < GROUPS)
        return jnp.where(hit, 1.0, 0.0).astype(BF)

    sq_b = iota((B, B), 0) == iota((B, B), 1)
    ctx_col = jnp.sum(
        jnp.where(sq_b, jnp.broadcast_to(ctx_row, (B, B)), 0).astype(F32), axis=1, keepdims=True
    )
    lane_b = iota((B, 128), 1)
    freq = (lane_b & 31).astype(F32)
    angle = ctx_col * jnp.exp(freq * (-2.0 * math.log(ROPE_BASE) / HEAD_DIM))
    cosine = jnp.cos(angle)
    sine = jnp.sin(angle)
    front = (lane_b & 63) < 32
    sine = jnp.where(front, -sine, sine)

    def rotate(v):
        turned = jnp.where(front, pltpu.roll(v, 96, 1), pltpu.roll(v, 32, 1))
        return (v * cosine + turned * sine).astype(BF).astype(F32)

    inq[r] = jnp.zeros((ROWS, 128), BF)
    ret[r] = jnp.zeros((ROWS, 128), BF)
    wq_v[GROUPS * HEAD_DIM :, :] = jnp.zeros((HEAD_DIM, D), BF)
    wo_v[GROUPS * HEAD_DIM :, :] = jnp.zeros((HEAD_DIM, D), BF)
    router_v[EXPERTS:, :] = jnp.zeros((128 - EXPERTS, D), BF)
    get_wq.wait()
    get_wkv.wait()

    arrived(xg, rsem, 0)
    normed = xg[...].astype(F32).reshape(T * 8, H).astype(BF)
    q_all = [mm_t(normed, wq_v[:, c * H : (c + 1) * H]) for c in range(2)]
    kv_all = [mm(normed, wkv_v[c * H : (c + 1) * H, :]) for c in range(2)]
    q01 = rotate(unfold(q_all[0][:, 0:128], q_all[1][:, 0:128], T))
    q2 = rotate(unfold(q_all[0][:, 128:256], q_all[1][:, 128:256], T))
    new_kv = unfold(kv_all[0], kv_all[1], T)
    head_lane = lane_b < 64
    heads = [
        jnp.where(head_lane, q01, 0.0),
        jnp.where(head_lane, pltpu.roll(q01, 64, 1), 0.0),
        jnp.where(head_lane, q2, 0.0),
    ]
    marker = jnp.where(head_lane, 0.0, 1.0)
    qg_v[...] = jnp.concatenate(heads + [marker], axis=0).astype(BF)

    msg[...] = mm(a1_v[NL:, :], qg_v[...]).reshape(R, ROWS, 128).astype(BF)
    pl.semaphore_wait(ready, NZ - 1)
    exchange(msg, inq, 1)

    get_cache.wait()
    loc_v[0 : LOCAL * 8, :] = page_rows(
        mm(a1_v[0 : LOCAL * 8, :], qg_v[...]), cache_v[0:LOCAL]
    )
    if NL > LOCAL * 8:
        loc_v[LOCAL * 8 :, :] = jnp.zeros((NL - LOCAL * 8, 128), BF)
    eye = (iota((4 * B, 4 * B), 0) == iota((4 * B, 4 * B), 1)).astype(F32).astype(BF)
    owned_loc = mm_t(eye, a1_v[0:NL, :])[0:NR] > 0.5
    owned_in = mm_t(eye, a1_v[NL:, :])[0:NR] > 0.5
    lane_sel = iota((NR, 128), 1)
    max_sel = jnp.where((lane_sel == 0) | (lane_sel == 16), 1.0, 0.0).astype(BF)
    new_key = rotate(new_kv)
    new_score = jnp.concatenate(
        [jnp.sum(h * new_key, axis=1, keepdims=True) for h in heads], axis=0
    ) * ATTN_SCALE
    fresh = jnp.where(head_lane, 1.0, new_kv.astype(BF).astype(F32))
    fresh = jnp.concatenate([fresh] * GROUPS, axis=0)
    loc = loc_v[...]
    score_loc = jnp.where(owned_loc, mm_t(max_sel, loc), NEG_FILL)
    top_loc = jnp.maximum(new_score, jnp.max(score_loc, axis=1, keepdims=True))
    sum_loc = mm(jnp.exp(score_loc - top_loc).astype(BF), loc)
    sum_loc = sum_loc + jnp.exp(new_score - top_loc) * fresh
    fetch = fetch_map()
    place = place_map()

    arrived(inq, rsem, 1)
    sent = inq[...].astype(F32).reshape(NIN, 128).astype(BF)
    lent = page_rows(mm(fetch, sent), cache_v[LOCAL:POOL])
    ret_s[...] = mm(place, lent).reshape(R, ROWS, 128).astype(BF)
    exchange(ret_s, ret, 2)

    get_win.wait()
    win_f[...] = win_v[...].astype(F32)
    wgu_v[:, 0:UNITS] = win_f[pl.ds(0, D, stride=2), :].astype(BF)
    wgu_v[:, UNITS:] = win_f[pl.ds(1, D, stride=2), :].astype(BF)
    get_wo.wait()
    get_wdown.wait()
    get_router.wait()
    get_routes.wait()
    get_fgain.wait()
    eye_b = sq_b.astype(F32).astype(BF)
    chosen = mm_t(eye_b, routes_v[...].astype(F32).astype(BF))
    expert = iota((B, 128), 1)
    expert_f = expert.astype(F32)
    picked = jnp.zeros((B, 128), F32)
    for k in range(routes.shape[0]):
        picked = jnp.where(expert_f == chosen[:, k : k + 1], 1.0, picked)
    mine = expert == (t * UNITS) // FF
    gain_f = fold_gain(fgain_v)
    residual = fold_v[...]

    arrived(ret, rsem, 2)
    back = ret[...].astype(F32).reshape(NIN, 128).astype(BF)
    score_in = jnp.where(owned_in, mm_t(max_sel, back), NEG_FILL)
    top = jnp.maximum(top_loc, jnp.max(score_in, axis=1, keepdims=True))
    merged = jnp.exp(top_loc - top) * sum_loc + mm(jnp.exp(score_in - top).astype(BF), back)
    attention = (merged / merged[:, 32:33]).astype(BF).astype(F32)
    att0, att1, att2 = (attention[g * B : (g + 1) * B] for g in range(GROUPS))
    left = jnp.where(head_lane, pltpu.roll(att0, 64, 1), att1)
    right = jnp.where(head_lane, pltpu.roll(att2, 64, 1), 0.0)
    left1, left2 = expand(left, T)
    right1, right2 = expand(right, T)
    rows1 = jnp.concatenate([left1, right1], axis=1)
    rows2 = jnp.concatenate([left2, right2], axis=1)
    partial = mm(rows1, wo_v[:, 0:H]) + mm(rows2, wo_v[:, H:D])
    partial = partial.reshape(T, 8, H).astype(BF)
    rs_s[...] = partial
    scatter(rs_s, rs, 3)
    rs[t] = rs_s[t]
    arrived(rs, rsem, 3)
    summed = jnp.sum(rs[...].astype(F32), axis=0)
    attended = (residual + RESID_SCALE * summed).astype(BF)
    attended_f = attended.astype(F32)
    fg[t] = normalise(attended_f, gain_f).astype(BF)
    share(fg, 4)
    both_o[:, 0:H] = attended_f[0:4].astype(BF)
    both_o[:, H:D] = attended_f[4:8].astype(BF)

    arrived(fg, rsem, 4)
    ffn = fg[...].astype(F32).reshape(T * 8, H).astype(BF)
    up_all = [mm(ffn, wgu_v[c * H : (c + 1) * H, :]) for c in range(2)]
    log_all = [mm_t(ffn, router_v[:, c * H : (c + 1) * H]) for c in range(2)]
    gate = unfold(up_all[0][:, 0:UNITS], up_all[1][:, 0:UNITS], T)
    up = unfold(up_all[0][:, UNITS:], up_all[1][:, UNITS:], T)
    logits = jnp.where(picked > 0.0, unfold(log_all[0], log_all[1], T), NEG_FILL)
    chances = jnp.exp(logits - jnp.max(logits, axis=1, keepdims=True))
    chances = jnp.where(picked > 0.0, chances, 0.0)
    share_of = jnp.sum(jnp.where(mine, chances, 0.0), axis=1, keepdims=True) / jnp.sum(
        chances, axis=1, keepdims=True
    )
    active = gate * (1.0 / (1.0 + jnp.exp(-gate))) * up * share_of
    act1, act2 = expand(active, T)
    down = mm(act1, wdown_v[:, 0:H]) + mm(act2, wdown_v[:, H:D])
    es_s[...] = down.reshape(T, 8, H).astype(BF)
    scatter(es_s, es, 5)
    es[t] = es_s[t]
    arrived(es, rsem, 5)
    experts = jnp.sum(es[...].astype(F32), axis=0)
    both_o[:, D : D + H] = experts[0:4].astype(BF)
    both_o[:, D + H :] = experts[4:8].astype(BF)
    for phase, buf in enumerate((xg, inq, ret, rs, fg, es)):
        arrived(buf, ssem, phase)


def on_device(
    hidden,
    attn_gain,
    w_query,
    w_keyvalue,
    w_output,
    cache,
    page_table,
    ctx_len,
    move_dest,
    ffn_gain,
    router,
    routes,
    w_in,
    w_down,
):
    R = lax.axis_size("replica")
    T = lax.axis_size("tensor")
    D = hidden.shape[1]
    H = D // 2
    B = page_table.shape[0]
    POOL = cache.shape[0]
    OUT = move_dest.shape[0]
    LOCAL = POOL - OUT
    UNITS = w_down.shape[0]
    NL = -(-LOCAL * 8 // 128) * 128
    NIN = R * ROWS
    args = (
        hidden,
        attn_gain,
        w_query.T,
        w_keyvalue.reshape(D, 2 * HEAD_DIM),
        w_output,
        cache.reshape(POOL, PAGE, 2 * HEAD_DIM),
        page_table.T,
        ctx_len.reshape(1, B),
        move_dest.reshape(1, OUT),
        ffn_gain,
        router.T,
        routes.T,
        w_in.reshape(2 * D, UNITS),
        w_down,
    )
    vm = pltpu.VMEM
    landing = [vm(a.shape, a.dtype) for a in args]
    landing[2] = vm((256, D), BF)
    landing[4] = vm((256, D), BF)
    landing[10] = vm((128, D), BF)
    any_spec = pl.BlockSpec(memory_space=pltpu.HBM)
    group = vm((T, 8, H), BF)
    inbox = vm((R, ROWS, 128), BF)
    scratch = landing + [
        vm((2 * D, UNITS), F32),
        vm((D, 2 * UNITS), BF),
        vm((8, H), F32),
        vm((NL + NIN, 4 * B), BF),
        vm((4 * B, 128), BF),
        vm((NL, 128), BF),
        group,
        inbox,
        inbox,
        inbox,
        inbox,
        group,
        group,
        group,
        group,
        group,
        pltpu.SemaphoreType.DMA((len(args),)),
        pltpu.SemaphoreType.REGULAR,
        pltpu.SemaphoreType.DMA((6,)),
        pltpu.SemaphoreType.DMA((6,)),
    ]
    both = pl.pallas_call(
        functools.partial(kernel, R, T, B, NL, LOCAL, POOL, OUT, UNITS),
        out_shape=pltpu.VMEM((4, 2 * D), BF),
        in_specs=[any_spec] * len(args),
        out_specs=pl.BlockSpec(memory_space=pltpu.VMEM),
        scratch_shapes=scratch,
        name="decode_step",
        compiler_params=pltpu.CompilerParams(
            collective_id=0, has_side_effects=True, vmem_limit_bytes=32 * 1024 * 1024
        ),
    )(*[pltpu.with_memory_space_constraint(a, pltpu.HBM) for a in args])
    return both[:, 0:D], both[:, D:]


def solution(mesh):
    placed = (
        P(("replica", "tensor"), None),
        P(),
        P(None, "tensor"),
        P(None, "tensor", None),
        P("tensor", None),
        P("replica", None, "tensor", None),
        P("replica", None),
        P("replica"),
        P("replica"),
        P(),
        P(),
        P("replica", None),
        P(None, None, "tensor"),
        P("tensor", None),
    )
    return jax.shard_map(
        on_device,
        mesh=mesh,
        in_specs=placed,
        out_specs=(P(("replica", "tensor"), None), P(("replica", "tensor"), None)),
        check_vma=False,
    )
```

```python
import functools
import math

import jax
import jax.numpy as jnp
from jax import lax
from jax.experimental import pallas as pl
from jax.experimental.pallas import tpu as pltpu
from jax.sharding import PartitionSpec as P

HEAD_DIM = 64
EXPERTS = 40
FF = 512
CAP = 2
PAGE = 128
GROUPS = 3
ROWS = 8

ATTN_SCALE = 0.015625
RESID_SCALE = 0.22
ROPE_BASE = 10000.0
EPSILON = 1e-06
NEG_FILL = -1e30

BF = jnp.bfloat16
F32 = jnp.float32
I32 = jnp.int32
MESH = pl.DeviceIdType.MESH


def iota(shape, axis):
    return lax.broadcasted_iota(I32, shape, axis)


def mm(a, b):
    return lax.dot_general(a, b, (((1,), (0,)), ((), ())), preferred_element_type=F32)


def mm_t(a, b):
    return lax.dot_general(a, b, (((1,), (1,)), ((), ())), preferred_element_type=F32)


def roll4(v):
    return pltpu.roll(v, 4, 0)


def unfold(p0, p1, tensors):
    low = iota((8, p0.shape[1]), 0) < 4
    parts = []
    for a in range(tensors // 2):
        lo = p0[16 * a : 16 * a + 8] + roll4(p1[16 * a : 16 * a + 8])
        hi = roll4(p0[16 * a + 8 : 16 * a + 16]) + p1[16 * a + 8 : 16 * a + 16]
        parts.append(jnp.where(low, lo, hi))
    return jnp.concatenate(parts, axis=0)


def expand(v, tensors):
    low = iota((8, v.shape[1]), 0) < 4
    first, second = [], []
    for a in range(tensors // 2):
        piece = v[8 * a : 8 * a + 8]
        turned = roll4(piece)
        first.append(jnp.where(low, piece, 0.0))
        second.append(jnp.where(low, 0.0, turned))
        first.append(jnp.where(low, turned, 0.0))
        second.append(jnp.where(low, 0.0, piece))
    return jnp.concatenate(first, axis=0).astype(BF), jnp.concatenate(second, axis=0).astype(BF)


def page_rows(q_rows, pages):
    count = pages.shape[0]
    lane = iota((count * 8, 128), 1)
    span = jnp.where(lane < 64, pltpu.roll(q_rows, 64, 1), q_rows)
    query = jnp.where(lane < 64, q_rows, 0.0).reshape(count, 8, 128).astype(BF)
    scores = lax.dot_general(
        query, pages, (((2,), (2,)), ((0,), (0,))), preferred_element_type=F32
    ).reshape(count * 8, 128) * ATTN_SCALE
    in_range = lane.astype(F32) < span
    scores = jnp.where(in_range, scores, NEG_FILL)
    top = jnp.max(scores, axis=1, keepdims=True)
    weights = jnp.where(in_range, jnp.exp(scores - top), 0.0)
    total = jnp.sum(weights, axis=1, keepdims=True)
    out = lax.dot_general(
        weights.reshape(count, 8, 128).astype(BF),
        pages,
        (((2,), (1,)), ((0,), (0,))),
        preferred_element_type=F32,
    ).reshape(count * 8, 128)
    coarse = top.astype(BF).astype(F32)
    rows = jnp.where(
        lane < 16, coarse, jnp.where(lane < 32, top - coarse, jnp.where(lane < 64, total, out))
    )
    return rows.astype(BF)


def kernel(
    R, T, B, NL, LOCAL, POOL, OUT, UNITS,
    hid, again, wq, wkv, wo, cache, ptab, ctx, mdest, fgain, router, routes, win, wdown,
    both_o,
    hid_v, again_v, wq_v, wkv_v, wo_v, cache_v, ptab_v, ctx_v, mdest_v, fgain_v, router_v,
    routes_v, win_v, wdown_v, win_f, wgu_v, fold_v, a1_v, qg_v, loc_v,
    xg, msg, inq, ret_s, ret, rs_s, rs, fg, es_s, es,
    isem, ready, ssem, rsem,
):
    r = lax.axis_index("replica")
    t = lax.axis_index("tensor")
    D = hid.shape[1]
    H = D // 2
    NZ = math.isqrt(R)
    y, z = r // NZ, lax.rem(r, NZ)
    NIN = R * ROWS
    NR = GROUPS * B

    loads = []

    def load(src, dst):
        copy = pltpu.make_async_copy(src, dst, isem.at[len(loads)])
        copy.start()
        loads.append(copy)
        return copy

    get_hid = load(hid, hid_v)
    get_again = load(again, again_v)

    barrier = pltpu.get_barrier_semaphore()
    for k in range(1, T):
        pl.semaphore_signal(barrier, inc=1, device_id=(r, lax.rem(t + k, T)), device_id_type=MESH)
    for k in range(1, NZ):
        pl.semaphore_signal(
            barrier, inc=1, device_id=(lax.rem(y + k, NZ) * NZ + z, t), device_id_type=MESH
        )
        pl.semaphore_signal(
            barrier, inc=1, device_id=(y * NZ + lax.rem(z + k, NZ), t), device_id_type=MESH
        )

    low8 = iota((8, H), 0) < 4

    def normalise(folded, gain):
        squares = jnp.sum(folded * folded, axis=1, keepdims=True)
        mean = (squares + roll4(jnp.broadcast_to(squares, (8, 128)))[:, 0:1]) * (1.0 / D)
        return folded * lax.rsqrt(mean + EPSILON) * gain

    def fold_gain(ref):
        left = jnp.broadcast_to(ref[0:H].reshape(1, H), (8, H))
        right = jnp.broadcast_to(ref[H:D].reshape(1, H), (8, H))
        return jnp.where(low8, left, right)

    get_hid.wait()
    get_again.wait()
    hidden = hid_v[...].astype(F32)
    fold_v[0:4, :] = hidden[:, 0:H]
    fold_v[4:8, :] = hidden[:, H:D]
    xg[t] = normalise(fold_v[...], fold_gain(again_v)).astype(BF)

    pl.semaphore_wait(barrier, (T - 1) + 2 * (NZ - 1))
    chip, core, chips = t // 2, lax.rem(t, 2), T // 2
    steps = sorted(range(chips), key=lambda d: (-min(d, chips - d), d))
    peers = [
        lax.rem(chip + d, chips) * 2 + (core if same else 1 - core)
        for d in steps
        for same in (1, 0)
        if d or not same
    ]

    def share(buf, phase):
        for peer in peers:
            pltpu.make_async_remote_copy(
                buf.at[t], buf.at[t], ssem.at[phase], rsem.at[phase],
                device_id=(r, peer), device_id_type=MESH,
            ).start()

    def scatter(src, dst, phase):
        for peer in peers:
            pltpu.make_async_remote_copy(
                src.at[peer], dst.at[t], ssem.at[phase], rsem.at[phase],
                device_id=(r, peer), device_id_type=MESH,
            ).start()

    offsets = sorted(
        ((dy, dz) for dy in range(NZ) for dz in range(NZ) if dy or dz),
        key=lambda d: -(min(d[0], NZ - d[0]) + min(d[1], NZ - d[1])),
    )

    def exchange(src, dst, phase):
        for dy, dz in offsets:
            peer = lax.rem(y + dy, NZ) * NZ + lax.rem(z + dz, NZ)
            pltpu.make_async_remote_copy(
                src.at[peer], dst.at[r], ssem.at[phase], rsem.at[phase],
                device_id=(peer, t), device_id_type=MESH,
            ).start()

    def arrived(buf, sems, phase):
        part = buf.at[0 : buf.shape[0] - 1]
        pltpu.make_async_copy(part, part, sems.at[phase]).wait()

    share(xg, 0)
    for k in range(1, NZ):
        pl.semaphore_signal(
            ready, inc=1, device_id=(y * NZ + lax.rem(z + k, NZ), t), device_id_type=MESH
        )
    get_ptab = load(ptab, ptab_v)
    get_ctx = load(ctx, ctx_v)
    get_mdest = load(mdest, mdest_v)
    get_wq = load(wq, wq_v.at[0 : GROUPS * HEAD_DIM])
    get_wkv = load(wkv, wkv_v)
    get_cache = load(cache, cache_v)
    get_win = load(win, win_v)
    get_wo = load(wo, wo_v.at[0 : GROUPS * HEAD_DIM])
    get_wdown = load(wdown, wdown_v)
    get_router = load(router, router_v.at[0:EXPERTS])
    get_routes = load(routes, routes_v)
    get_fgain = load(fgain, fgain_v)

    get_ptab.wait()
    get_ctx.wait()
    get_mdest.wait()
    table = ptab_v[...]
    slots = table.shape[0]
    ctx_row = ctx_v[...]
    spans = jnp.where(
        table >= 0, jnp.clip(ctx_row - iota((slots, B), 0) * PAGE, 0, PAGE), 0
    )
    tile = (iota((B, 4 * B), 0) == (iota((B, 4 * B), 1) & (B - 1))).astype(F32).astype(BF)
    table_w = mm(table.astype(F32).astype(BF), tile)
    spans_w = mm(spans.astype(F32).astype(BF), tile)
    CH = 64 if NL % 64 == 0 and NIN % 64 == 0 else 32

    def claims(base, page, head):
        found = jnp.zeros((CH, 4 * B), F32)
        pages = page.astype(F32)
        for k in range(slots):
            found = found + jnp.where(pages == table_w[k : k + 1, :], spans_w[k : k + 1, :], 0.0)
        group = iota((CH, 4 * B), 1) // B
        flag = jnp.where((group == head) & (found > 0.0), 1.0, 0.0)
        rows = jnp.where(group == GROUPS, found, flag)
        a1_v[pl.ds(base, CH), :] = jnp.where(head < GROUPS, rows, 0.0).astype(BF)

    def local_claims(c, carry):
        row = iota((CH, 4 * B), 0) + c * CH
        page = jnp.where(row < LOCAL * 8, row >> 3, -2)
        claims(pl.multiple_of(c * CH, CH), page, row & 7)
        return carry

    def inbox_claims(c, carry):
        row = iota((CH, 4 * B), 0) + c * CH
        claims(pl.multiple_of(NL + c * CH, CH), POOL + (row >> 2), row & 3)
        return carry

    lax.fori_loop(0, NL // CH, local_claims, 0)
    lax.fori_loop(0, NIN // CH, inbox_claims, 0)

    dest_row = mdest_v[...]
    dest_sq = jnp.broadcast_to(dest_row, (OUT, OUT))
    sub_sq, lane_sq = iota((OUT, OUT), 0), iota((OUT, OUT), 1)
    dest_col = jnp.sum(jnp.where(sub_sq == lane_sq, dest_sq, 0).astype(F32), axis=1, keepdims=True)
    dest_f = dest_sq.astype(F32)
    earlier = (dest_col == dest_f) & (sub_sq < lane_sq)
    rank = jnp.sum(jnp.where(earlier, 1.0, 0.0), axis=0, keepdims=True)
    slot_row = dest_f * CAP + rank
    slot_sq = slot_row[0:8, :]
    NQ = OUT * 8
    grow = (iota((OUT, NQ), 0) == (iota((OUT, NQ), 1) >> 3)).astype(F32).astype(BF)
    slot_lane = mm(slot_sq.astype(BF), grow)[0:1, :]
    pick = iota((NQ, OUT), 1) == (iota((NQ, OUT), 0) >> 3)
    slot_sub = jnp.sum(
        jnp.where(pick, jnp.broadcast_to(slot_row[0:1, :], (NQ, OUT)), 0.0), axis=1, keepdims=True
    )

    def fetch_map():
        row, lane = iota((NQ, NIN), 0), iota((NQ, NIN), 1)
        same = (lane >> 2).astype(F32) == slot_sub
        hit = same & ((row & 7) == (lane & 3)) & ((lane & 3) < GROUPS)
        return jnp.where(hit, 1.0, 0.0).astype(BF)

    def place_map():
        row, lane = iota((NIN, NQ), 0), iota((NIN, NQ), 1)
        same = (row >> 2).astype(F32) == slot_lane
        hit = same & ((lane & 7) == (row & 3)) & ((row & 3) < GROUPS)
        return jnp.where(hit, 1.0, 0.0).astype(BF)

    sq_b = iota((B, B), 0) == iota((B, B), 1)
    ctx_col = jnp.sum(
        jnp.where(sq_b, jnp.broadcast_to(ctx_row, (B, B)), 0).astype(F32), axis=1, keepdims=True
    )
    lane_b = iota((B, 128), 1)
    freq = (lane_b & 31).astype(F32)
    angle = ctx_col * jnp.exp(freq * (-2.0 * math.log(ROPE_BASE) / HEAD_DIM))
    cosine = jnp.cos(angle)
    sine = jnp.sin(angle)
    front = (lane_b & 63) < 32
    sine = jnp.where(front, -sine, sine)

    def rotate(v):
        turned = jnp.where(front, pltpu.roll(v, 96, 1), pltpu.roll(v, 32, 1))
        return (v * cosine + turned * sine).astype(BF).astype(F32)

    inq[r] = jnp.zeros((ROWS, 128), BF)
    ret[r] = jnp.zeros((ROWS, 128), BF)
    wq_v[GROUPS * HEAD_DIM :, :] = jnp.zeros((HEAD_DIM, D), BF)
    wo_v[GROUPS * HEAD_DIM :, :] = jnp.zeros((HEAD_DIM, D), BF)
    router_v[EXPERTS:, :] = jnp.zeros((128 - EXPERTS, D), BF)
    get_wq.wait()
    get_wkv.wait()

    arrived(xg, rsem, 0)
    normed = xg[...].astype(F32).reshape(T * 8, H).astype(BF)
    q_all = [mm_t(normed, wq_v[:, c * H : (c + 1) * H]) for c in range(2)]
    kv_all = [mm(normed, wkv_v[c * H : (c + 1) * H, :]) for c in range(2)]
    q01 = rotate(unfold(q_all[0][:, 0:128], q_all[1][:, 0:128], T))
    q2 = rotate(unfold(q_all[0][:, 128:256], q_all[1][:, 128:256], T))
    new_kv = unfold(kv_all[0], kv_all[1], T)
    head_lane = lane_b < 64
    heads = [
        jnp.where(head_lane, q01, 0.0),
        jnp.where(head_lane, pltpu.roll(q01, 64, 1), 0.0),
        jnp.where(head_lane, q2, 0.0),
    ]
    marker = jnp.where(head_lane, 0.0, 1.0)
    qg_v[...] = jnp.concatenate(heads + [marker], axis=0).astype(BF)

    msg[...] = mm(a1_v[NL:, :], qg_v[...]).reshape(R, ROWS, 128).astype(BF)
    pl.semaphore_wait(ready, NZ - 1)
    exchange(msg, inq, 1)

    get_cache.wait()
    loc_v[0 : LOCAL * 8, :] = page_rows(
        mm(a1_v[0 : LOCAL * 8, :], qg_v[...]), cache_v[0:LOCAL]
    )
    if NL > LOCAL * 8:
        loc_v[LOCAL * 8 :, :] = jnp.zeros((NL - LOCAL * 8, 128), BF)
    eye = (iota((4 * B, 4 * B), 0) == iota((4 * B, 4 * B), 1)).astype(F32).astype(BF)
    owned_loc = mm_t(eye, a1_v[0:NL, :])[0:NR] > 0.5
    owned_in = mm_t(eye, a1_v[NL:, :])[0:NR] > 0.5
    lane_sel = iota((NR, 128), 1)
    max_sel = jnp.where((lane_sel == 0) | (lane_sel == 16), 1.0, 0.0).astype(BF)
    new_key = rotate(new_kv)
    new_score = jnp.concatenate(
        [jnp.sum(h * new_key, axis=1, keepdims=True) for h in heads], axis=0
    ) * ATTN_SCALE
    fresh = jnp.where(head_lane, 1.0, new_kv.astype(BF).astype(F32))
    fresh = jnp.concatenate([fresh] * GROUPS, axis=0)
    loc = loc_v[...]
    score_loc = jnp.where(owned_loc, mm_t(max_sel, loc), NEG_FILL)
    top_loc = jnp.maximum(new_score, jnp.max(score_loc, axis=1, keepdims=True))
    sum_loc = mm(jnp.exp(score_loc - top_loc).astype(BF), loc)
    sum_loc = sum_loc + jnp.exp(new_score - top_loc) * fresh
    fetch = fetch_map()
    place = place_map()

    arrived(inq, rsem, 1)
    sent = inq[...].astype(F32).reshape(NIN, 128).astype(BF)
    lent = page_rows(mm(fetch, sent), cache_v[LOCAL:POOL])
    ret_s[...] = mm(place, lent).reshape(R, ROWS, 128).astype(BF)
    exchange(ret_s, ret, 2)

    get_win.wait()
    win_f[...] = win_v[...].astype(F32)
    wgu_v[:, 0:UNITS] = win_f[pl.ds(0, D, stride=2), :].astype(BF)
    wgu_v[:, UNITS:] = win_f[pl.ds(1, D, stride=2), :].astype(BF)
    get_wo.wait()
    get_wdown.wait()
    get_router.wait()
    get_routes.wait()
    get_fgain.wait()
    eye_b = sq_b.astype(F32).astype(BF)
    chosen = mm_t(eye_b, routes_v[...].astype(F32).astype(BF))
    expert = iota((B, 128), 1)
    expert_f = expert.astype(F32)
    picked = jnp.zeros((B, 128), F32)
    for k in range(routes.shape[0]):
        picked = jnp.where(expert_f == chosen[:, k : k + 1], 1.0, picked)
    mine = expert == (t * UNITS) // FF
    gain_f = fold_gain(fgain_v)
    residual = fold_v[...]

    arrived(ret, rsem, 2)
    back = ret[...].astype(F32).reshape(NIN, 128).astype(BF)
    score_in = jnp.where(owned_in, mm_t(max_sel, back), NEG_FILL)
    top = jnp.maximum(top_loc, jnp.max(score_in, axis=1, keepdims=True))
    merged = jnp.exp(top_loc - top) * sum_loc + mm(jnp.exp(score_in - top).astype(BF), back)
    attention = (merged / merged[:, 32:33]).astype(BF).astype(F32)
    att0, att1, att2 = (attention[g * B : (g + 1) * B] for g in range(GROUPS))
    left = jnp.where(head_lane, pltpu.roll(att0, 64, 1), att1)
    right = jnp.where(head_lane, pltpu.roll(att2, 64, 1), 0.0)
    left1, left2 = expand(left, T)
    right1, right2 = expand(right, T)
    rows1 = jnp.concatenate([left1, right1], axis=1)
    rows2 = jnp.concatenate([left2, right2], axis=1)
    partial = mm(rows1, wo_v[:, 0:H]) + mm(rows2, wo_v[:, H:D])
    partial = partial.reshape(T, 8, H).astype(BF)
    rs_s[...] = partial
    scatter(rs_s, rs, 3)
    rs[t] = rs_s[t]
    arrived(rs, rsem, 3)
    summed = jnp.sum(rs[...].astype(F32), axis=0)
    attended = (residual + RESID_SCALE * summed).astype(BF)
    attended_f = attended.astype(F32)
    fg[t] = normalise(attended_f, gain_f).astype(BF)
    share(fg, 4)
    both_o[:, 0:H] = attended_f[0:4].astype(BF)
    both_o[:, H:D] = attended_f[4:8].astype(BF)

    arrived(fg, rsem, 4)
    ffn = fg[...].astype(F32).reshape(T * 8, H).astype(BF)
    up_all = [mm(ffn, wgu_v[c * H : (c + 1) * H, :]) for c in range(2)]
    log_all = [mm_t(ffn, router_v[:, c * H : (c + 1) * H]) for c in range(2)]
    gate = unfold(up_all[0][:, 0:UNITS], up_all[1][:, 0:UNITS], T)
    up = unfold(up_all[0][:, UNITS:], up_all[1][:, UNITS:], T)
    logits = jnp.where(picked > 0.0, unfold(log_all[0], log_all[1], T), NEG_FILL)
    chances = jnp.exp(logits - jnp.max(logits, axis=1, keepdims=True))
    chances = jnp.where(picked > 0.0, chances, 0.0)
    share_of = jnp.sum(jnp.where(mine, chances, 0.0), axis=1, keepdims=True) / jnp.sum(
        chances, axis=1, keepdims=True
    )
    active = gate * (1.0 / (1.0 + jnp.exp(-gate))) * up * share_of
    act1, act2 = expand(active, T)
    down = mm(act1, wdown_v[:, 0:H]) + mm(act2, wdown_v[:, H:D])
    es_s[...] = down.reshape(T, 8, H).astype(BF)
    scatter(es_s, es, 5)
    es[t] = es_s[t]
    arrived(es, rsem, 5)
    experts = jnp.sum(es[...].astype(F32), axis=0)
    both_o[:, D : D + H] = experts[0:4].astype(BF)
    both_o[:, D + H :] = experts[4:8].astype(BF)
    for phase, buf in enumerate((xg, inq, ret, rs, fg, es)):
        arrived(buf, ssem, phase)


def on_device(
    hidden,
    attn_gain,
    w_query,
    w_keyvalue,
    w_output,
    cache,
    page_table,
    ctx_len,
    move_dest,
    ffn_gain,
    router,
    routes,
    w_in,
    w_down,
):
    R = lax.axis_size("replica")
    T = lax.axis_size("tensor")
    D = hidden.shape[1]
    H = D // 2
    B = page_table.shape[0]
    POOL = cache.shape[0]
    OUT = move_dest.shape[0]
    LOCAL = POOL - OUT
    UNITS = w_down.shape[0]
    NL = -(-LOCAL * 8 // 128) * 128
    NIN = R * ROWS
    args = (
        hidden,
        attn_gain,
        w_query.T,
        w_keyvalue.reshape(D, 2 * HEAD_DIM),
        w_output,
        cache.reshape(POOL, PAGE, 2 * HEAD_DIM),
        page_table.T,
        ctx_len.reshape(1, B),
        move_dest.reshape(1, OUT),
        ffn_gain,
        router.T,
        routes.T,
        w_in.reshape(2 * D, UNITS),
        w_down,
    )
    vm = pltpu.VMEM
    landing = [vm(a.shape, a.dtype) for a in args]
    landing[2] = vm((256, D), BF)
    landing[4] = vm((256, D), BF)
    landing[10] = vm((128, D), BF)
    any_spec = pl.BlockSpec(memory_space=pltpu.HBM)
    group = vm((T, 8, H), BF)
    inbox = vm((R, ROWS, 128), BF)
    scratch = landing + [
        vm((2 * D, UNITS), F32),
        vm((D, 2 * UNITS), BF),
        vm((8, H), F32),
        vm((NL + NIN, 4 * B), BF),
        vm((4 * B, 128), BF),
        vm((NL, 128), BF),
        group,
        inbox,
        inbox,
        inbox,
        inbox,
        group,
        group,
        group,
        group,
        group,
        pltpu.SemaphoreType.DMA((len(args),)),
        pltpu.SemaphoreType.REGULAR,
        pltpu.SemaphoreType.DMA((6,)),
        pltpu.SemaphoreType.DMA((6,)),
    ]
    both = pl.pallas_call(
        functools.partial(kernel, R, T, B, NL, LOCAL, POOL, OUT, UNITS),
        out_shape=pltpu.VMEM((4, 2 * D), BF),
        in_specs=[any_spec] * len(args),
        out_specs=pl.BlockSpec(memory_space=pltpu.VMEM),
        scratch_shapes=scratch,
        name="decode_step",
        compiler_params=pltpu.CompilerParams(
            collective_id=0, has_side_effects=True, vmem_limit_bytes=32 * 1024 * 1024
        ),
    )(*[pltpu.with_memory_space_constraint(a, pltpu.HBM) for a in args])
    return both[:, 0:D], both[:, D:]


def solution(mesh):
    placed = (
        P(("replica", "tensor"), None),
        P(),
        P(None, "tensor"),
        P(None, "tensor", None),
        P("tensor", None),
        P("replica", None, "tensor", None),
        P("replica", None),
        P("replica"),
        P("replica"),
        P(),
        P(),
        P("replica", None),
        P(None, None, "tensor"),
        P("tensor", None),
    )
    return jax.shard_map(
        on_device,
        mesh=mesh,
        in_specs=placed,
        out_specs=(P(("replica", "tensor"), None), P(("replica", "tensor"), None)),
        check_vma=False,
    )
```

```python
import functools
import math

import jax
import jax.numpy as jnp
from jax import lax
from jax.experimental import pallas as pl
from jax.experimental.pallas import tpu as pltpu
from jax.sharding import PartitionSpec as P

HEAD_DIM = 64
EXPERTS = 40
FF = 512
CAP = 2
PAGE = 128
GROUPS = 3
ROWS = 8

ATTN_SCALE = 0.015625
RESID_SCALE = 0.22
ROPE_BASE = 10000.0
EPSILON = 1e-06
NEG_FILL = -1e30

BF = jnp.bfloat16
F32 = jnp.float32
I32 = jnp.int32
MESH = pl.DeviceIdType.MESH


def iota(shape, axis):
    return lax.broadcasted_iota(I32, shape, axis)


def mm(a, b):
    return lax.dot_general(a, b, (((1,), (0,)), ((), ())), preferred_element_type=F32)


def mm_t(a, b):
    return lax.dot_general(a, b, (((1,), (1,)), ((), ())), preferred_element_type=F32)


def roll4(v):
    return pltpu.roll(v, 4, 0)


def unfold(p0, p1, tensors):
    low = iota((8, p0.shape[1]), 0) < 4
    parts = []
    for a in range(tensors // 2):
        lo = p0[16 * a : 16 * a + 8] + roll4(p1[16 * a : 16 * a + 8])
        hi = roll4(p0[16 * a + 8 : 16 * a + 16]) + p1[16 * a + 8 : 16 * a + 16]
        parts.append(jnp.where(low, lo, hi))
    return jnp.concatenate(parts, axis=0)


def expand(v, tensors):
    low = iota((8, v.shape[1]), 0) < 4
    first, second = [], []
    for a in range(tensors // 2):
        piece = v[8 * a : 8 * a + 8]
        turned = roll4(piece)
        first.append(jnp.where(low, piece, 0.0))
        second.append(jnp.where(low, 0.0, turned))
        first.append(jnp.where(low, turned, 0.0))
        second.append(jnp.where(low, 0.0, piece))
    return jnp.concatenate(first, axis=0).astype(BF), jnp.concatenate(second, axis=0).astype(BF)


def page_rows(q_rows, pages):
    count = pages.shape[0]
    lane = iota((count * 8, 128), 1)
    span = jnp.where(lane < 64, pltpu.roll(q_rows, 64, 1), q_rows)
    query = jnp.where(lane < 64, q_rows, 0.0).reshape(count, 8, 128).astype(BF)
    scores = lax.dot_general(
        query, pages, (((2,), (2,)), ((0,), (0,))), preferred_element_type=F32
    ).reshape(count * 8, 128) * ATTN_SCALE
    in_range = lane.astype(F32) < span
    scores = jnp.where(in_range, scores, NEG_FILL)
    top = jnp.max(scores, axis=1, keepdims=True)
    weights = jnp.where(in_range, jnp.exp(scores - top), 0.0)
    total = jnp.sum(weights, axis=1, keepdims=True)
    out = lax.dot_general(
        weights.reshape(count, 8, 128).astype(BF),
        pages,
        (((2,), (1,)), ((0,), (0,))),
        preferred_element_type=F32,
    ).reshape(count * 8, 128)
    coarse = top.astype(BF).astype(F32)
    middle = (top - coarse).astype(BF).astype(F32)
    fine = top - coarse - middle
    rows = jnp.where(lane < 16, middle, jnp.where(lane < 32, fine, jnp.where(lane < 64, total, out)))
    rows = jnp.where(lane < 8, coarse, rows)
    return rows.astype(BF)


def kernel(
    R, T, B, NL, LOCAL, POOL, OUT, UNITS,
    hid, again, wq, wkv, wo, cache, ptab, ctx, mdest, fgain, router, routes, win, wdown,
    both_o,
    hid_v, again_v, wq_v, wkv_v, wo_v, cache_v, ptab_v, ctx_v, mdest_v, fgain_v, router_v,
    routes_v, win_v, wdown_v, win_f, wgu_v, fold_v, a1_v, qg_v, loc_v,
    xg, msg, inq, ret_s, ret, rs_s, rs, fg, es_s, es,
    isem, ready, ssem, rsem,
):
    r = lax.axis_index("replica")
    t = lax.axis_index("tensor")
    D = hid.shape[1]
    H = D // 2
    NZ = math.isqrt(R)
    y, z = r // NZ, lax.rem(r, NZ)
    NIN = R * ROWS
    NR = GROUPS * B

    loads = []

    def load(src, dst):
        copy = pltpu.make_async_copy(src, dst, isem.at[len(loads)])
        copy.start()
        loads.append(copy)
        return copy

    get_hid = load(hid, hid_v)
    get_again = load(again, again_v)

    barrier = pltpu.get_barrier_semaphore()
    for k in range(1, T):
        pl.semaphore_signal(barrier, inc=1, device_id=(r, lax.rem(t + k, T)), device_id_type=MESH)
    ring = sorted(range(1, NZ), key=lambda d: -min(d, NZ - d))
    for k in ring:
        pl.semaphore_signal(
            barrier, inc=1, device_id=(lax.rem(y + k, NZ) * NZ + z, t), device_id_type=MESH
        )
        pl.semaphore_signal(
            barrier, inc=1, device_id=(y * NZ + lax.rem(z + k, NZ), t), device_id_type=MESH
        )

    low8 = iota((8, H), 0) < 4

    def normalise(folded, gain):
        squares = jnp.sum(folded * folded, axis=1, keepdims=True)
        mean = (squares + roll4(jnp.broadcast_to(squares, (8, 128)))[:, 0:1]) * (1.0 / D)
        return folded * lax.rsqrt(mean + EPSILON) * gain

    def fold_gain(ref):
        left = jnp.broadcast_to(ref[0:H].reshape(1, H), (8, H))
        right = jnp.broadcast_to(ref[H:D].reshape(1, H), (8, H))
        return jnp.where(low8, left, right)

    get_hid.wait()
    get_again.wait()
    hidden = hid_v[...].astype(F32)
    fold_v[0:4, :] = hidden[:, 0:H]
    fold_v[4:8, :] = hidden[:, H:D]
    xg[t] = normalise(fold_v[...], fold_gain(again_v)).astype(BF)

    pl.semaphore_wait(barrier, (T - 1) + 2 * (NZ - 1))
    chip, core, chips = t // 2, lax.rem(t, 2), T // 2
    steps = sorted(range(chips), key=lambda d: (-min(d, chips - d), d))
    peers = [
        lax.rem(chip + d, chips) * 2 + (core if same else 1 - core)
        for d in steps
        for same in (1, 0)
        if d or not same
    ]

    def share(buf, phase):
        for peer in peers:
            pltpu.make_async_remote_copy(
                buf.at[t], buf.at[t], ssem.at[phase], rsem.at[phase],
                device_id=(r, peer), device_id_type=MESH,
            ).start()

    def scatter(src, dst, phase):
        for peer in peers:
            pltpu.make_async_remote_copy(
                src.at[peer], dst.at[t], ssem.at[phase], rsem.at[phase],
                device_id=(r, peer), device_id_type=MESH,
            ).start()

    offsets = sorted(
        ((dy, dz) for dy in range(NZ) for dz in range(NZ) if dy or dz),
        key=lambda d: -(min(d[0], NZ - d[0]) + min(d[1], NZ - d[1])),
    )

    def exchange(src, dst, phase):
        for dy, dz in offsets:
            peer = lax.rem(y + dy, NZ) * NZ + lax.rem(z + dz, NZ)
            pltpu.make_async_remote_copy(
                src.at[peer], dst.at[r], ssem.at[phase], rsem.at[phase],
                device_id=(peer, t), device_id_type=MESH,
            ).start()

    def arrived(buf, sems, phase):
        part = buf.at[0 : buf.shape[0] - 1]
        pltpu.make_async_copy(part, part, sems.at[phase]).wait()

    for k in ring:
        pl.semaphore_signal(
            ready, inc=1, device_id=(y * NZ + lax.rem(z + k, NZ), t), device_id_type=MESH
        )
    share(xg, 0)
    get_ptab = load(ptab, ptab_v)
    get_ctx = load(ctx, ctx_v)
    get_mdest = load(mdest, mdest_v)
    get_wq = load(wq, wq_v.at[0 : GROUPS * HEAD_DIM])
    get_wkv = load(wkv, wkv_v)
    get_cache = load(cache, cache_v)
    get_win = load(win, win_v)
    get_wo = load(wo, wo_v.at[0 : GROUPS * HEAD_DIM])
    get_wdown = load(wdown, wdown_v)
    get_router = load(router, router_v.at[0:EXPERTS])
    get_routes = load(routes, routes_v)
    get_fgain = load(fgain, fgain_v)

    get_ptab.wait()
    get_ctx.wait()
    get_mdest.wait()
    table = ptab_v[...]
    slots = table.shape[0]
    ctx_row = ctx_v[...]
    spans = jnp.where(
        table >= 0, jnp.clip(ctx_row - iota((slots, B), 0) * PAGE, 0, PAGE), 0
    )
    tile = (iota((B, 4 * B), 0) == (iota((B, 4 * B), 1) & (B - 1))).astype(F32).astype(BF)
    table_w = mm(table.astype(F32).astype(BF), tile)
    spans_w = mm(spans.astype(F32).astype(BF), tile)
    CH = 64 if NL % 64 == 0 and NIN % 64 == 0 else 32

    def claims(base, page, head):
        found = jnp.zeros((CH, 4 * B), F32)
        pages = page.astype(F32)
        for k in range(slots):
            found = found + jnp.where(pages == table_w[k : k + 1, :], spans_w[k : k + 1, :], 0.0)
        group = iota((CH, 4 * B), 1) // B
        flag = jnp.where((group == head) & (found > 0.0), 1.0, 0.0)
        rows = jnp.where(group == GROUPS, found, flag)
        a1_v[pl.ds(base, CH), :] = jnp.where(head < GROUPS, rows, 0.0).astype(BF)

    def local_claims(c, carry):
        row = iota((CH, 4 * B), 0) + c * CH
        page = jnp.where(row < LOCAL * 8, row >> 3, -2)
        claims(pl.multiple_of(c * CH, CH), page, row & 7)
        return carry

    def inbox_claims(c, carry):
        row = iota((CH, 4 * B), 0) + c * CH
        claims(pl.multiple_of(NL + c * CH, CH), POOL + (row >> 2), row & 3)
        return carry

    lax.fori_loop(0, NL // CH, local_claims, 0)
    lax.fori_loop(0, NIN // CH, inbox_claims, 0)

    dest_row = mdest_v[...]
    dest_sq = jnp.broadcast_to(dest_row, (OUT, OUT))
    sub_sq, lane_sq = iota((OUT, OUT), 0), iota((OUT, OUT), 1)
    dest_col = jnp.sum(jnp.where(sub_sq == lane_sq, dest_sq, 0).astype(F32), axis=1, keepdims=True)
    dest_f = dest_sq.astype(F32)
    earlier = (dest_col == dest_f) & (sub_sq < lane_sq)
    rank = jnp.sum(jnp.where(earlier, 1.0, 0.0), axis=0, keepdims=True)
    slot_row = dest_f * CAP + rank
    slot_sq = slot_row[0:8, :]
    NQ = OUT * 8
    grow = (iota((OUT, NQ), 0) == (iota((OUT, NQ), 1) >> 3)).astype(F32).astype(BF)
    slot_lane = mm(slot_sq.astype(BF), grow)[0:1, :]
    pick = iota((NQ, OUT), 1) == (iota((NQ, OUT), 0) >> 3)
    slot_sub = jnp.sum(
        jnp.where(pick, jnp.broadcast_to(slot_row[0:1, :], (NQ, OUT)), 0.0), axis=1, keepdims=True
    )

    def fetch_map():
        row, lane = iota((NQ, NIN), 0), iota((NQ, NIN), 1)
        same = (lane >> 2).astype(F32) == slot_sub
        hit = same & ((row & 7) == (lane & 3)) & ((lane & 3) < GROUPS)
        return jnp.where(hit, 1.0, 0.0).astype(BF)

    def place_map():
        row, lane = iota((NIN, NQ), 0), iota((NIN, NQ), 1)
        same = (row >> 2).astype(F32) == slot_lane
        hit = same & ((lane & 7) == (row & 3)) & ((row & 3) < GROUPS)
        return jnp.where(hit, 1.0, 0.0).astype(BF)

    sq_b = iota((B, B), 0) == iota((B, B), 1)
    ctx_col = jnp.sum(
        jnp.where(sq_b, jnp.broadcast_to(ctx_row, (B, B)), 0).astype(F32), axis=1, keepdims=True
    )
    lane_b = iota((B, 128), 1)
    freq = (lane_b & 31).astype(F32)
    angle = ctx_col * jnp.exp(freq * (-2.0 * math.log(ROPE_BASE) / HEAD_DIM))
    cosine = jnp.cos(angle)
    sine = jnp.sin(angle)
    front = (lane_b & 63) < 32
    sine = jnp.where(front, -sine, sine)

    def rotate(v):
        turned = jnp.where(front, pltpu.roll(v, 96, 1), pltpu.roll(v, 32, 1))
        return (v * cosine + turned * sine).astype(BF).astype(F32)

    inq[r] = jnp.zeros((ROWS, 128), BF)
    ret[r] = jnp.zeros((ROWS, 128), BF)
    wq_v[GROUPS * HEAD_DIM :, :] = jnp.zeros((HEAD_DIM, D), BF)
    wo_v[GROUPS * HEAD_DIM :, :] = jnp.zeros((HEAD_DIM, D), BF)
    router_v[EXPERTS:, :] = jnp.zeros((128 - EXPERTS, D), BF)
    get_wq.wait()
    get_wkv.wait()

    arrived(xg, rsem, 0)
    normed = xg[...].reshape(T * 8, H)
    q_all = [mm_t(normed, wq_v[:, c * H : (c + 1) * H]) for c in range(2)]
    kv_all = [mm(normed, wkv_v[c * H : (c + 1) * H, :]) for c in range(2)]
    q01 = rotate(unfold(q_all[0][:, 0:128], q_all[1][:, 0:128], T))
    q2 = rotate(unfold(q_all[0][:, 128:256], q_all[1][:, 128:256], T))
    new_kv = unfold(kv_all[0], kv_all[1], T)
    head_lane = lane_b < 64
    heads = [
        jnp.where(head_lane, q01, 0.0),
        jnp.where(head_lane, pltpu.roll(q01, 64, 1), 0.0),
        jnp.where(head_lane, q2, 0.0),
    ]
    marker = jnp.where(head_lane, 0.0, 1.0)
    qg_v[...] = jnp.concatenate(heads + [marker], axis=0).astype(BF)

    msg[...] = mm(a1_v[NL:, :], qg_v[...]).reshape(R, ROWS, 128).astype(BF)
    pl.semaphore_wait(ready, NZ - 1)
    exchange(msg, inq, 1)

    get_cache.wait()
    loc_v[0 : LOCAL * 8, :] = page_rows(
        mm(a1_v[0 : LOCAL * 8, :], qg_v[...]), cache_v[0:LOCAL]
    )
    if NL > LOCAL * 8:
        loc_v[LOCAL * 8 :, :] = jnp.zeros((NL - LOCAL * 8, 128), BF)
    eye = (iota((4 * B, 4 * B), 0) == iota((4 * B, 4 * B), 1)).astype(F32).astype(BF)
    owned_loc = mm_t(eye, a1_v[0:NL, :])[0:NR] > 0.5
    owned_in = mm_t(eye, a1_v[NL:, :])[0:NR] > 0.5
    lane_sel = iota((NR, 128), 1)
    max_sel = jnp.where((lane_sel == 0) | (lane_sel == 8) | (lane_sel == 16), 1.0, 0.0).astype(BF)
    new_key = rotate(new_kv)
    new_score = jnp.concatenate(
        [jnp.sum(h * new_key, axis=1, keepdims=True) for h in heads], axis=0
    ) * ATTN_SCALE
    fresh = jnp.where(head_lane, 1.0, new_kv.astype(BF).astype(F32))
    fresh = jnp.concatenate([fresh] * GROUPS, axis=0)
    loc = loc_v[...]
    score_loc = jnp.where(owned_loc, mm_t(max_sel, loc), NEG_FILL)
    top_loc = jnp.maximum(new_score, jnp.max(score_loc, axis=1, keepdims=True))
    sum_loc = mm(jnp.exp(score_loc - top_loc).astype(BF), loc)
    sum_loc = sum_loc + jnp.exp(new_score - top_loc) * fresh
    fetch = fetch_map()
    place = place_map()

    arrived(inq, rsem, 1)
    sent = inq[...].reshape(NIN, 128)
    lent = page_rows(mm(fetch, sent), cache_v[LOCAL:POOL])
    ret_s[...] = mm(place, lent).reshape(R, ROWS, 128).astype(BF)
    exchange(ret_s, ret, 2)

    get_win.wait()
    win_f[...] = win_v[...].astype(F32)
    wgu_v[:, 0:UNITS] = win_f[pl.ds(0, D, stride=2), :].astype(BF)
    wgu_v[:, UNITS:] = win_f[pl.ds(1, D, stride=2), :].astype(BF)
    get_wo.wait()
    get_wdown.wait()
    get_router.wait()
    get_routes.wait()
    get_fgain.wait()
    eye_b = sq_b.astype(F32).astype(BF)
    chosen = mm_t(eye_b, routes_v[...].astype(F32).astype(BF))
    expert = iota((B, 128), 1)
    expert_f = expert.astype(F32)
    picked = jnp.zeros((B, 128), F32)
    for k in range(routes.shape[0]):
        picked = jnp.where(expert_f == chosen[:, k : k + 1], 1.0, picked)
    mine = expert == (t * UNITS) // FF
    gain_f = fold_gain(fgain_v)
    residual = fold_v[...]

    arrived(ret, rsem, 2)
    back = ret[...].reshape(NIN, 128)
    score_in = jnp.where(owned_in, mm_t(max_sel, back), NEG_FILL)
    top = jnp.maximum(top_loc, jnp.max(score_in, axis=1, keepdims=True))
    merged = jnp.exp(top_loc - top) * sum_loc + mm(jnp.exp(score_in - top).astype(BF), back)
    attention = (merged / merged[:, 32:33]).astype(BF).astype(F32)
    att0, att1, att2 = (attention[g * B : (g + 1) * B] for g in range(GROUPS))
    left = jnp.where(head_lane, pltpu.roll(att0, 64, 1), att1)
    right = jnp.where(head_lane, pltpu.roll(att2, 64, 1), 0.0)
    left1, left2 = expand(left, T)
    right1, right2 = expand(right, T)
    rows1 = jnp.concatenate([left1, right1], axis=1)
    rows2 = jnp.concatenate([left2, right2], axis=1)
    partial = mm(rows1, wo_v[:, 0:H]) + mm(rows2, wo_v[:, H:D])
    partial = partial.reshape(T, 8, H).astype(BF)
    rs_s[...] = partial
    scatter(rs_s, rs, 3)
    rs[t] = rs_s[t]
    arrived(rs, rsem, 3)
    summed = jnp.sum(rs[...].astype(F32), axis=0)
    attended = (residual + RESID_SCALE * summed).astype(BF)
    attended_f = attended.astype(F32)
    fg[t] = normalise(attended_f, gain_f).astype(BF)
    share(fg, 4)
    both_o[:, 0:H] = attended_f[0:4].astype(BF)
    both_o[:, H:D] = attended_f[4:8].astype(BF)

    arrived(fg, rsem, 4)
    ffn = fg[...].reshape(T * 8, H)
    up_all = [mm(ffn, wgu_v[c * H : (c + 1) * H, :]) for c in range(2)]
    log_all = [mm_t(ffn, router_v[:, c * H : (c + 1) * H]) for c in range(2)]
    gate = unfold(up_all[0][:, 0:UNITS], up_all[1][:, 0:UNITS], T)
    up = unfold(up_all[0][:, UNITS:], up_all[1][:, UNITS:], T)
    logits = jnp.where(picked > 0.0, unfold(log_all[0], log_all[1], T), NEG_FILL)
    chances = jnp.exp(logits - jnp.max(logits, axis=1, keepdims=True))
    chances = jnp.where(picked > 0.0, chances, 0.0)
    share_of = jnp.sum(jnp.where(mine, chances, 0.0), axis=1, keepdims=True) / jnp.sum(
        chances, axis=1, keepdims=True
    )
    active = gate * (1.0 / (1.0 + jnp.exp(-gate))) * up * share_of
    act1, act2 = expand(active, T)
    down = mm(act1, wdown_v[:, 0:H]) + mm(act2, wdown_v[:, H:D])
    es_s[...] = down.reshape(T, 8, H).astype(BF)
    scatter(es_s, es, 5)
    es[t] = es_s[t]
    arrived(es, rsem, 5)
    experts = jnp.sum(es[...].astype(F32), axis=0)
    both_o[:, D : D + H] = experts[0:4].astype(BF)
    both_o[:, D + H :] = experts[4:8].astype(BF)
    for phase, buf in enumerate((xg, inq, ret, rs, fg, es)):
        arrived(buf, ssem, phase)


def on_device(
    hidden,
    attn_gain,
    w_query,
    w_keyvalue,
    w_output,
    cache,
    page_table,
    ctx_len,
    move_dest,
    ffn_gain,
    router,
    routes,
    w_in,
    w_down,
):
    R = lax.axis_size("replica")
    T = lax.axis_size("tensor")
    D = hidden.shape[1]
    H = D // 2
    B = page_table.shape[0]
    POOL = cache.shape[0]
    OUT = move_dest.shape[0]
    LOCAL = POOL - OUT
    UNITS = w_down.shape[0]
    NL = -(-LOCAL * 8 // 128) * 128
    NIN = R * ROWS
    args = (
        hidden,
        attn_gain,
        w_query.T,
        w_keyvalue.reshape(D, 2 * HEAD_DIM),
        w_output,
        cache.reshape(POOL, PAGE, 2 * HEAD_DIM),
        page_table.T,
        ctx_len.reshape(1, B),
        move_dest.reshape(1, OUT),
        ffn_gain,
        router.T,
        routes.T,
        w_in.reshape(2 * D, UNITS),
        w_down,
    )
    vm = pltpu.VMEM
    landing = [vm(a.shape, a.dtype) for a in args]
    landing[2] = vm((256, D), BF)
    landing[4] = vm((256, D), BF)
    landing[10] = vm((128, D), BF)
    any_spec = pl.BlockSpec(memory_space=pltpu.HBM)
    group = vm((T, 8, H), BF)
    inbox = vm((R, ROWS, 128), BF)
    scratch = landing + [
        vm((2 * D, UNITS), F32),
        vm((D, 2 * UNITS), BF),
        vm((8, H), F32),
        vm((NL + NIN, 4 * B), BF),
        vm((4 * B, 128), BF),
        vm((NL, 128), BF),
        group,
        inbox,
        inbox,
        inbox,
        inbox,
        group,
        group,
        group,
        group,
        group,
        pltpu.SemaphoreType.DMA((len(args),)),
        pltpu.SemaphoreType.REGULAR,
        pltpu.SemaphoreType.DMA((6,)),
        pltpu.SemaphoreType.DMA((6,)),
    ]
    both = pl.pallas_call(
        functools.partial(kernel, R, T, B, NL, LOCAL, POOL, OUT, UNITS),
        out_shape=pltpu.VMEM((4, 2 * D), BF),
        in_specs=[any_spec] * len(args),
        out_specs=pl.BlockSpec(memory_space=pltpu.VMEM),
        scratch_shapes=scratch,
        name="decode_step",
        compiler_params=pltpu.CompilerParams(
            collective_id=0, has_side_effects=True, vmem_limit_bytes=32 * 1024 * 1024
        ),
    )(*[pltpu.with_memory_space_constraint(a, pltpu.HBM) for a in args])
    return both[:, 0:D], both[:, D:]


def solution(mesh):
    placed = (
        P(("replica", "tensor"), None),
        P(),
        P(None, "tensor"),
        P(None, "tensor", None),
        P("tensor", None),
        P("replica", None, "tensor", None),
        P("replica", None),
        P("replica"),
        P("replica"),
        P(),
        P(),
        P("replica", None),
        P(None, None, "tensor"),
        P("tensor", None),
    )
    return jax.shard_map(
        on_device,
        mesh=mesh,
        in_specs=placed,
        out_specs=(P(("replica", "tensor"), None), P(("replica", "tensor"), None)),
        check_vma=False,
    )
```

```python
import functools
import math

import jax
import jax.numpy as jnp
from jax import lax
from jax.experimental import pallas as pl
from jax.experimental.pallas import tpu as pltpu
from jax.sharding import PartitionSpec as P

HEAD_DIM = 64
EXPERTS = 40
FF = 512
CAP = 2
PAGE = 128
GROUPS = 3
ROWS = 8

ATTN_SCALE = 0.015625
RESID_SCALE = 0.22
ROPE_BASE = 10000.0
EPSILON = 1e-06
NEG_FILL = -1e30

BF = jnp.bfloat16
F32 = jnp.float32
I32 = jnp.int32
MESH = pl.DeviceIdType.MESH


def iota(shape, axis):
    return lax.broadcasted_iota(I32, shape, axis)


def mm(a, b):
    return lax.dot_general(a, b, (((1,), (0,)), ((), ())), preferred_element_type=F32)


def mm_t(a, b):
    return lax.dot_general(a, b, (((1,), (1,)), ((), ())), preferred_element_type=F32)


def roll4(v):
    return pltpu.roll(v, 4, 0)


def unfold(p0, p1, tensors):
    low = iota((8, p0.shape[1]), 0) < 4
    parts = []
    for a in range(tensors // 2):
        lo = p0[16 * a : 16 * a + 8] + roll4(p1[16 * a : 16 * a + 8])
        hi = roll4(p0[16 * a + 8 : 16 * a + 16]) + p1[16 * a + 8 : 16 * a + 16]
        parts.append(jnp.where(low, lo, hi))
    return jnp.concatenate(parts, axis=0)


def expand(v, tensors):
    low = iota((8, v.shape[1]), 0) < 4
    first, second = [], []
    for a in range(tensors // 2):
        piece = v[8 * a : 8 * a + 8]
        turned = roll4(piece)
        first.append(jnp.where(low, piece, 0.0))
        second.append(jnp.where(low, 0.0, turned))
        first.append(jnp.where(low, turned, 0.0))
        second.append(jnp.where(low, 0.0, piece))
    return jnp.concatenate(first, axis=0).astype(BF), jnp.concatenate(second, axis=0).astype(BF)


def page_rows(q_rows, pages):
    count = pages.shape[0]
    lane = iota((count * 8, 128), 1)
    span = jnp.where(lane < 64, pltpu.roll(q_rows, 64, 1), q_rows)
    query = jnp.where(lane < 64, q_rows, 0.0).reshape(count, 8, 128).astype(BF)
    scores = lax.dot_general(
        query, pages, (((2,), (2,)), ((0,), (0,))), preferred_element_type=F32
    ).reshape(count * 8, 128) * ATTN_SCALE
    in_range = lane.astype(F32) < span
    scores = jnp.where(in_range, scores, NEG_FILL)
    top = jnp.max(scores, axis=1, keepdims=True)
    weights = jnp.where(in_range, jnp.exp(scores - top), 0.0)
    total = jnp.sum(weights, axis=1, keepdims=True)
    out = lax.dot_general(
        weights.reshape(count, 8, 128).astype(BF),
        pages,
        (((2,), (1,)), ((0,), (0,))),
        preferred_element_type=F32,
    ).reshape(count * 8, 128)
    coarse = top.astype(BF).astype(F32)
    middle = (top - coarse).astype(BF).astype(F32)
    fine = top - coarse - middle
    rows = jnp.where(lane < 16, middle, jnp.where(lane < 32, fine, jnp.where(lane < 64, total, out)))
    rows = jnp.where(lane < 8, coarse, rows)
    return rows.astype(BF)


def kernel(
    R, T, B, NL, LOCAL, POOL, OUT, UNITS,
    hid, again, wq, wkv, wo, cache, ptab, ctx, mdest, fgain, router, routes, win, wdown,
    both_o,
    hid_v, again_v, wq_v, wkv_v, wo_v, cache_v, ptab_v, ctx_v, mdest_v, fgain_v, router_v,
    routes_v, win_v, wdown_v, win_f, wgu_v, fold_v, a1_v, qg_v, loc_v,
    xg, msg, inq, ret_s, ret, rs_s, rs, fg, es_s, es,
    isem, ready, ssem, rsem,
):
    r = lax.axis_index("replica")
    t = lax.axis_index("tensor")
    D = hid.shape[1]
    H = D // 2
    NZ = math.isqrt(R)
    y, z = r // NZ, lax.rem(r, NZ)
    NIN = R * ROWS
    NR = GROUPS * B

    loads = []

    def load(src, dst):
        copy = pltpu.make_async_copy(src, dst, isem.at[len(loads)])
        copy.start()
        loads.append(copy)
        return copy

    get_hid = load(hid, hid_v)
    get_again = load(again, again_v)

    barrier = pltpu.get_barrier_semaphore()
    ring = sorted(range(1, NZ), key=lambda d: -min(d, NZ - d))
    for k in ring:
        pl.semaphore_signal(
            barrier, inc=1, device_id=(lax.rem(y + k, NZ) * NZ + z, t), device_id_type=MESH
        )
    for k in ring:
        pl.semaphore_signal(
            barrier, inc=1, device_id=(y * NZ + lax.rem(z + k, NZ), t), device_id_type=MESH
        )
    for k in range(1, T):
        pl.semaphore_signal(barrier, inc=1, device_id=(r, lax.rem(t + k, T)), device_id_type=MESH)

    low8 = iota((8, H), 0) < 4

    def normalise(folded, gain):
        squares = jnp.sum(folded * folded, axis=1, keepdims=True)
        mean = (squares + roll4(jnp.broadcast_to(squares, (8, 128)))[:, 0:1]) * (1.0 / D)
        return folded * lax.rsqrt(mean + EPSILON) * gain

    def fold_gain(ref):
        left = jnp.broadcast_to(ref[0:H].reshape(1, H), (8, H))
        right = jnp.broadcast_to(ref[H:D].reshape(1, H), (8, H))
        return jnp.where(low8, left, right)

    get_hid.wait()
    get_again.wait()
    hidden = hid_v[...].astype(F32)
    fold_v[0:4, :] = hidden[:, 0:H]
    fold_v[4:8, :] = hidden[:, H:D]
    xg[t] = normalise(fold_v[...], fold_gain(again_v)).astype(BF)

    pl.semaphore_wait(barrier, (T - 1) + 2 * (NZ - 1))
    chip, core, chips = t // 2, lax.rem(t, 2), T // 2
    steps = sorted(range(chips), key=lambda d: (-min(d, chips - d), d))
    peers = [
        lax.rem(chip + d, chips) * 2 + (core if same else 1 - core)
        for d in steps
        for same in (1, 0)
        if d or not same
    ]

    def share(buf, phase):
        for peer in peers:
            pltpu.make_async_remote_copy(
                buf.at[t], buf.at[t], ssem.at[phase], rsem.at[phase],
                device_id=(r, peer), device_id_type=MESH,
            ).start()

    def scatter(src, dst, phase):
        for peer in peers:
            pltpu.make_async_remote_copy(
                src.at[peer], dst.at[t], ssem.at[phase], rsem.at[phase],
                device_id=(r, peer), device_id_type=MESH,
            ).start()

    offsets = sorted(
        ((dy, dz) for dy in range(NZ) for dz in range(NZ) if dy or dz),
        key=lambda d: -(min(d[0], NZ - d[0]) + min(d[1], NZ - d[1])),
    )

    def exchange(src, dst, phase):
        for dy, dz in offsets:
            peer = lax.rem(y + dy, NZ) * NZ + lax.rem(z + dz, NZ)
            pltpu.make_async_remote_copy(
                src.at[peer], dst.at[r], ssem.at[phase], rsem.at[phase],
                device_id=(peer, t), device_id_type=MESH,
            ).start()

    def arrived(buf, sems, phase):
        part = buf.at[0 : buf.shape[0] - 1]
        pltpu.make_async_copy(part, part, sems.at[phase]).wait()

    share(xg, 0)
    for k in range(1, NZ):
        pl.semaphore_signal(
            ready, inc=1, device_id=(y * NZ + lax.rem(z + k, NZ), t), device_id_type=MESH
        )
    get_ptab = load(ptab, ptab_v)
    get_ctx = load(ctx, ctx_v)
    get_mdest = load(mdest, mdest_v)
    get_wq = load(wq, wq_v.at[0 : GROUPS * HEAD_DIM])
    get_wkv = load(wkv, wkv_v)
    get_cache = load(cache, cache_v)
    get_win = load(win, win_v)
    get_wo = load(wo, wo_v.at[0 : GROUPS * HEAD_DIM])
    get_wdown = load(wdown, wdown_v)
    get_router = load(router, router_v.at[0:EXPERTS])
    get_routes = load(routes, routes_v)
    get_fgain = load(fgain, fgain_v)

    get_ptab.wait()
    get_ctx.wait()
    get_mdest.wait()
    table = ptab_v[...]
    slots = table.shape[0]
    ctx_row = ctx_v[...]
    spans = jnp.where(
        table >= 0, jnp.clip(ctx_row - iota((slots, B), 0) * PAGE, 0, PAGE), 0
    )
    tile = (iota((B, 4 * B), 0) == (iota((B, 4 * B), 1) & (B - 1))).astype(F32).astype(BF)
    table_w = mm(table.astype(F32).astype(BF), tile)
    spans_w = mm(spans.astype(F32).astype(BF), tile)
    CH = 64 if NL % 64 == 0 and NIN % 64 == 0 else 32

    def claims(base, page, head):
        found = jnp.zeros((CH, 4 * B), F32)
        pages = page.astype(F32)
        for k in range(slots):
            found = found + jnp.where(pages == table_w[k : k + 1, :], spans_w[k : k + 1, :], 0.0)
        group = iota((CH, 4 * B), 1) // B
        flag = jnp.where((group == head) & (found > 0.0), 1.0, 0.0)
        rows = jnp.where(group == GROUPS, found, flag)
        a1_v[pl.ds(base, CH), :] = jnp.where(head < GROUPS, rows, 0.0).astype(BF)

    def local_claims(c, carry):
        row = iota((CH, 4 * B), 0) + c * CH
        page = jnp.where(row < LOCAL * 8, row >> 3, -2)
        claims(pl.multiple_of(c * CH, CH), page, row & 7)
        return carry

    def inbox_claims(c, carry):
        row = iota((CH, 4 * B), 0) + c * CH
        claims(pl.multiple_of(NL + c * CH, CH), POOL + (row >> 2), row & 3)
        return carry

    lax.fori_loop(0, NL // CH, local_claims, 0)
    lax.fori_loop(0, NIN // CH, inbox_claims, 0)

    dest_row = mdest_v[...]
    dest_sq = jnp.broadcast_to(dest_row, (OUT, OUT))
    sub_sq, lane_sq = iota((OUT, OUT), 0), iota((OUT, OUT), 1)
    dest_col = jnp.sum(jnp.where(sub_sq == lane_sq, dest_sq, 0).astype(F32), axis=1, keepdims=True)
    dest_f = dest_sq.astype(F32)
    earlier = (dest_col == dest_f) & (sub_sq < lane_sq)
    rank = jnp.sum(jnp.where(earlier, 1.0, 0.0), axis=0, keepdims=True)
    slot_row = dest_f * CAP + rank
    slot_sq = slot_row[0:8, :]
    NQ = OUT * 8
    grow = (iota((OUT, NQ), 0) == (iota((OUT, NQ), 1) >> 3)).astype(F32).astype(BF)
    slot_lane = mm(slot_sq.astype(BF), grow)[0:1, :]
    pick = iota((NQ, OUT), 1) == (iota((NQ, OUT), 0) >> 3)
    slot_sub = jnp.sum(
        jnp.where(pick, jnp.broadcast_to(slot_row[0:1, :], (NQ, OUT)), 0.0), axis=1, keepdims=True
    )

    def fetch_map():
        row, lane = iota((NQ, NIN), 0), iota((NQ, NIN), 1)
        same = (lane >> 2).astype(F32) == slot_sub
        hit = same & ((row & 7) == (lane & 3)) & ((lane & 3) < GROUPS)
        return jnp.where(hit, 1.0, 0.0).astype(BF)

    def place_map():
        row, lane = iota((NIN, NQ), 0), iota((NIN, NQ), 1)
        same = (row >> 2).astype(F32) == slot_lane
        hit = same & ((lane & 7) == (row & 3)) & ((row & 3) < GROUPS)
        return jnp.where(hit, 1.0, 0.0).astype(BF)

    sq_b = iota((B, B), 0) == iota((B, B), 1)
    ctx_col = jnp.sum(
        jnp.where(sq_b, jnp.broadcast_to(ctx_row, (B, B)), 0).astype(F32), axis=1, keepdims=True
    )
    lane_b = iota((B, 128), 1)
    freq = (lane_b & 31).astype(F32)
    angle = ctx_col * jnp.exp(freq * (-2.0 * math.log(ROPE_BASE) / HEAD_DIM))
    cosine = jnp.cos(angle)
    sine = jnp.sin(angle)
    front = (lane_b & 63) < 32
    sine = jnp.where(front, -sine, sine)

    def rotate(v):
        turned = jnp.where(front, pltpu.roll(v, 96, 1), pltpu.roll(v, 32, 1))
        return (v * cosine + turned * sine).astype(BF).astype(F32)

    inq[r] = jnp.zeros((ROWS, 128), BF)
    ret[r] = jnp.zeros((ROWS, 128), BF)
    wq_v[GROUPS * HEAD_DIM :, :] = jnp.zeros((HEAD_DIM, D), BF)
    wo_v[GROUPS * HEAD_DIM :, :] = jnp.zeros((HEAD_DIM, D), BF)
    router_v[EXPERTS:, :] = jnp.zeros((128 - EXPERTS, D), BF)
    get_wq.wait()
    get_wkv.wait()

    arrived(xg, rsem, 0)
    normed = xg[...].astype(F32).reshape(T * 8, H).astype(BF)
    q_all = [mm_t(normed, wq_v[:, c * H : (c + 1) * H]) for c in range(2)]
    kv_all = [mm(normed, wkv_v[c * H : (c + 1) * H, :]) for c in range(2)]
    q01 = rotate(unfold(q_all[0][:, 0:128], q_all[1][:, 0:128], T))
    q2 = rotate(unfold(q_all[0][:, 128:256], q_all[1][:, 128:256], T))
    new_kv = unfold(kv_all[0], kv_all[1], T)
    head_lane = lane_b < 64
    heads = [
        jnp.where(head_lane, q01, 0.0),
        jnp.where(head_lane, pltpu.roll(q01, 64, 1), 0.0),
        jnp.where(head_lane, q2, 0.0),
    ]
    marker = jnp.where(head_lane, 0.0, 1.0)
    qg_v[...] = jnp.concatenate(heads + [marker], axis=0).astype(BF)

    msg[...] = mm(a1_v[NL:, :], qg_v[...]).reshape(R, ROWS, 128).astype(BF)
    pl.semaphore_wait(ready, NZ - 1)
    exchange(msg, inq, 1)

    get_cache.wait()
    loc_v[0 : LOCAL * 8, :] = page_rows(
        mm(a1_v[0 : LOCAL * 8, :], qg_v[...]), cache_v[0:LOCAL]
    )
    if NL > LOCAL * 8:
        loc_v[LOCAL * 8 :, :] = jnp.zeros((NL - LOCAL * 8, 128), BF)
    eye = (iota((4 * B, 4 * B), 0) == iota((4 * B, 4 * B), 1)).astype(F32).astype(BF)
    owned_loc = mm_t(eye, a1_v[0:NL, :])[0:NR] > 0.5
    owned_in = mm_t(eye, a1_v[NL:, :])[0:NR] > 0.5
    lane_sel = iota((NR, 128), 1)
    max_sel = jnp.where((lane_sel == 0) | (lane_sel == 8) | (lane_sel == 16), 1.0, 0.0).astype(BF)
    new_key = rotate(new_kv)
    new_score = jnp.concatenate(
        [jnp.sum(h * new_key, axis=1, keepdims=True) for h in heads], axis=0
    ) * ATTN_SCALE
    fresh = jnp.where(head_lane, 1.0, new_kv.astype(BF).astype(F32))
    fresh = jnp.concatenate([fresh] * GROUPS, axis=0)
    loc = loc_v[...]
    score_loc = jnp.where(owned_loc, mm_t(max_sel, loc), NEG_FILL)
    top_loc = jnp.maximum(new_score, jnp.max(score_loc, axis=1, keepdims=True))
    sum_loc = mm(jnp.exp(score_loc - top_loc).astype(BF), loc)
    sum_loc = sum_loc + jnp.exp(new_score - top_loc) * fresh
    fetch = fetch_map()
    place = place_map()

    arrived(inq, rsem, 1)
    sent = inq[...].astype(F32).reshape(NIN, 128).astype(BF)
    lent = page_rows(mm(fetch, sent), cache_v[LOCAL:POOL])
    ret_s[...] = mm(place, lent).reshape(R, ROWS, 128).astype(BF)
    exchange(ret_s, ret, 2)

    get_win.wait()
    win_f[...] = win_v[...].astype(F32)
    wgu_v[:, 0:UNITS] = win_f[pl.ds(0, D, stride=2), :].astype(BF)
    wgu_v[:, UNITS:] = win_f[pl.ds(1, D, stride=2), :].astype(BF)
    get_wo.wait()
    get_wdown.wait()
    get_router.wait()
    get_routes.wait()
    get_fgain.wait()
    eye_b = sq_b.astype(F32).astype(BF)
    chosen = mm_t(eye_b, routes_v[...].astype(F32).astype(BF))
    expert = iota((B, 128), 1)
    expert_f = expert.astype(F32)
    picked = jnp.zeros((B, 128), F32)
    for k in range(routes.shape[0]):
        picked = jnp.where(expert_f == chosen[:, k : k + 1], 1.0, picked)
    mine = expert == (t * UNITS) // FF
    gain_f = fold_gain(fgain_v)
    residual = fold_v[...]

    arrived(ret, rsem, 2)
    back = ret[...].astype(F32).reshape(NIN, 128).astype(BF)
    score_in = jnp.where(owned_in, mm_t(max_sel, back), NEG_FILL)
    top = jnp.maximum(top_loc, jnp.max(score_in, axis=1, keepdims=True))
    merged = jnp.exp(top_loc - top) * sum_loc + mm(jnp.exp(score_in - top).astype(BF), back)
    attention = (merged / merged[:, 32:33]).astype(BF).astype(F32)
    att0, att1, att2 = (attention[g * B : (g + 1) * B] for g in range(GROUPS))
    left = jnp.where(head_lane, pltpu.roll(att0, 64, 1), att1)
    right = jnp.where(head_lane, pltpu.roll(att2, 64, 1), 0.0)
    left1, left2 = expand(left, T)
    right1, right2 = expand(right, T)
    rows1 = jnp.concatenate([left1, right1], axis=1)
    rows2 = jnp.concatenate([left2, right2], axis=1)
    partial = mm(rows1, wo_v[:, 0:H]) + mm(rows2, wo_v[:, H:D])
    partial = partial.reshape(T, 8, H).astype(BF)
    rs_s[...] = partial
    scatter(rs_s, rs, 3)
    rs[t] = rs_s[t]
    arrived(rs, rsem, 3)
    summed = jnp.sum(rs[...].astype(F32), axis=0)
    attended = (residual + RESID_SCALE * summed).astype(BF)
    attended_f = attended.astype(F32)
    fg[t] = normalise(attended_f, gain_f).astype(BF)
    share(fg, 4)
    both_o[:, 0:H] = attended_f[0:4].astype(BF)
    both_o[:, H:D] = attended_f[4:8].astype(BF)

    arrived(fg, rsem, 4)
    ffn = fg[...].astype(F32).reshape(T * 8, H).astype(BF)
    up_all = [mm(ffn, wgu_v[c * H : (c + 1) * H, :]) for c in range(2)]
    log_all = [mm_t(ffn, router_v[:, c * H : (c + 1) * H]) for c in range(2)]
    gate = unfold(up_all[0][:, 0:UNITS], up_all[1][:, 0:UNITS], T)
    up = unfold(up_all[0][:, UNITS:], up_all[1][:, UNITS:], T)
    logits = jnp.where(picked > 0.0, unfold(log_all[0], log_all[1], T), NEG_FILL)
    chances = jnp.exp(logits - jnp.max(logits, axis=1, keepdims=True))
    chances = jnp.where(picked > 0.0, chances, 0.0)
    share_of = jnp.sum(jnp.where(mine, chances, 0.0), axis=1, keepdims=True) / jnp.sum(
        chances, axis=1, keepdims=True
    )
    active = gate * (1.0 / (1.0 + jnp.exp(-gate))) * up * share_of
    act1, act2 = expand(active, T)
    down = mm(act1, wdown_v[:, 0:H]) + mm(act2, wdown_v[:, H:D])
    es_s[...] = down.reshape(T, 8, H).astype(BF)
    scatter(es_s, es, 5)
    es[t] = es_s[t]
    arrived(es, rsem, 5)
    experts = jnp.sum(es[...].astype(F32), axis=0)
    both_o[:, D : D + H] = experts[0:4].astype(BF)
    both_o[:, D + H :] = experts[4:8].astype(BF)
    for phase, buf in enumerate((xg, inq, ret, rs, fg, es)):
        arrived(buf, ssem, phase)


def on_device(
    hidden,
    attn_gain,
    w_query,
    w_keyvalue,
    w_output,
    cache,
    page_table,
    ctx_len,
    move_dest,
    ffn_gain,
    router,
    routes,
    w_in,
    w_down,
):
    R = lax.axis_size("replica")
    T = lax.axis_size("tensor")
    D = hidden.shape[1]
    H = D // 2
    B = page_table.shape[0]
    POOL = cache.shape[0]
    OUT = move_dest.shape[0]
    LOCAL = POOL - OUT
    UNITS = w_down.shape[0]
    NL = -(-LOCAL * 8 // 128) * 128
    NIN = R * ROWS
    args = (
        hidden,
        attn_gain,
        w_query.T,
        w_keyvalue.reshape(D, 2 * HEAD_DIM),
        w_output,
        cache.reshape(POOL, PAGE, 2 * HEAD_DIM),
        page_table.T,
        ctx_len.reshape(1, B),
        move_dest.reshape(1, OUT),
        ffn_gain,
        router.T,
        routes.T,
        w_in.reshape(2 * D, UNITS),
        w_down,
    )
    vm = pltpu.VMEM
    landing = [vm(a.shape, a.dtype) for a in args]
    landing[2] = vm((256, D), BF)
    landing[4] = vm((256, D), BF)
    landing[10] = vm((128, D), BF)
    any_spec = pl.BlockSpec(memory_space=pltpu.HBM)
    group = vm((T, 8, H), BF)
    inbox = vm((R, ROWS, 128), BF)
    scratch = landing + [
        vm((2 * D, UNITS), F32),
        vm((D, 2 * UNITS), BF),
        vm((8, H), F32),
        vm((NL + NIN, 4 * B), BF),
        vm((4 * B, 128), BF),
        vm((NL, 128), BF),
        group,
        inbox,
        inbox,
        inbox,
        inbox,
        group,
        group,
        group,
        group,
        group,
        pltpu.SemaphoreType.DMA((len(args),)),
        pltpu.SemaphoreType.REGULAR,
        pltpu.SemaphoreType.DMA((6,)),
        pltpu.SemaphoreType.DMA((6,)),
    ]
    both = pl.pallas_call(
        functools.partial(kernel, R, T, B, NL, LOCAL, POOL, OUT, UNITS),
        out_shape=pltpu.VMEM((4, 2 * D), BF),
        in_specs=[any_spec] * len(args),
        out_specs=pl.BlockSpec(memory_space=pltpu.VMEM),
        scratch_shapes=scratch,
        name="decode_step",
        compiler_params=pltpu.CompilerParams(
            collective_id=0, has_side_effects=True, vmem_limit_bytes=32 * 1024 * 1024
        ),
    )(*[pltpu.with_memory_space_constraint(a, pltpu.HBM) for a in args])
    return both[:, 0:D], both[:, D:]


def solution(mesh):
    placed = (
        P(("replica", "tensor"), None),
        P(),
        P(None, "tensor"),
        P(None, "tensor", None),
        P("tensor", None),
        P("replica", None, "tensor", None),
        P("replica", None),
        P("replica"),
        P("replica"),
        P(),
        P(),
        P("replica", None),
        P(None, None, "tensor"),
        P("tensor", None),
    )
    return jax.shard_map(
        on_device,
        mesh=mesh,
        in_specs=placed,
        out_specs=(P(("replica", "tensor"), None), P(("replica", "tensor"), None)),
        check_vma=False,
    )
```

```python
import functools
import math

import jax
import jax.numpy as jnp
from jax import lax
from jax.experimental import pallas as pl
from jax.experimental.pallas import tpu as pltpu
from jax.sharding import PartitionSpec as P

HEAD_DIM = 64
EXPERTS = 40
FF = 512
CAP = 2
PAGE = 128
GROUPS = 3
ROWS = 8

ATTN_SCALE = 0.015625
RESID_SCALE = 0.22
ROPE_BASE = 10000.0
EPSILON = 1e-06
NEG_FILL = -1e30

BF = jnp.bfloat16
F32 = jnp.float32
I32 = jnp.int32
MESH = pl.DeviceIdType.MESH


def iota(shape, axis):
    return lax.broadcasted_iota(I32, shape, axis)


def mm(a, b):
    return lax.dot_general(a, b, (((1,), (0,)), ((), ())), preferred_element_type=F32)


def mm_t(a, b):
    return lax.dot_general(a, b, (((1,), (1,)), ((), ())), preferred_element_type=F32)


def roll4(v):
    return pltpu.roll(v, 4, 0)


def unfold(p0, p1, tensors):
    low = iota((8, p0.shape[1]), 0) < 4
    parts = []
    for a in range(tensors // 2):
        lo = p0[16 * a : 16 * a + 8] + roll4(p1[16 * a : 16 * a + 8])
        hi = roll4(p0[16 * a + 8 : 16 * a + 16]) + p1[16 * a + 8 : 16 * a + 16]
        parts.append(jnp.where(low, lo, hi))
    return jnp.concatenate(parts, axis=0)


def expand(v, tensors):
    low = iota((8, v.shape[1]), 0) < 4
    first, second = [], []
    for a in range(tensors // 2):
        piece = v[8 * a : 8 * a + 8]
        turned = roll4(piece)
        first.append(jnp.where(low, piece, 0.0))
        second.append(jnp.where(low, 0.0, turned))
        first.append(jnp.where(low, turned, 0.0))
        second.append(jnp.where(low, 0.0, piece))
    return jnp.concatenate(first, axis=0).astype(BF), jnp.concatenate(second, axis=0).astype(BF)


def page_rows(q_rows, pages, values):
    count = pages.shape[0]
    lane = iota((count * 8, 128), 1)
    span = jnp.where(lane < 64, pltpu.roll(q_rows, 64, 1), q_rows)
    query = jnp.where(lane < 64, q_rows, 0.0).reshape(count, 8, 128).astype(BF)
    scores = lax.dot_general(
        query, pages, (((2,), (2,)), ((0,), (0,))), preferred_element_type=F32
    ).reshape(count * 8, 128) * ATTN_SCALE
    in_range = lane.astype(F32) < span
    scores = jnp.where(in_range, scores, NEG_FILL)
    top = jnp.max(scores, axis=1, keepdims=True)
    weights = jnp.where(in_range, jnp.exp(scores - top), 0.0)
    out = lax.dot_general(
        weights.reshape(count, 8, 128).astype(BF),
        values,
        (((2,), (1,)), ((0,), (0,))),
        preferred_element_type=F32,
    ).reshape(count * 8, 128)
    coarse = top.astype(BF).astype(F32)
    middle = (top - coarse).astype(BF).astype(F32)
    fine = top - coarse - middle
    rows = jnp.where(lane < 16, middle, jnp.where(lane < 32, fine, out))
    rows = jnp.where(lane < 8, coarse, rows)
    return rows.astype(BF)


def kernel(
    R, T, B, NL, LOCAL, POOL, OUT, UNITS,
    hid, again, wq, wkv, wo, cache, ptab, ctx, mdest, fgain, router, routes, win, wdown,
    both_o,
    hid_v, again_v, wq_v, wkv_v, wo_v, cache_v, ptab_v, ctx_v, mdest_v, fgain_v, router_v,
    routes_v, win_v, wdown_v, win_f, wgu_v, fold_v, a1_v, qg_v, loc_v,
    values_v, xg, msg, inq, ret_s, ret, rs_s, rs, fg, es_s, es,
    isem, ready, ssem, rsem,
):
    r = lax.axis_index("replica")
    t = lax.axis_index("tensor")
    D = hid.shape[1]
    H = D // 2
    NZ = math.isqrt(R)
    y, z = r // NZ, lax.rem(r, NZ)
    NIN = R * ROWS
    NR = GROUPS * B

    loads = []

    def load(src, dst):
        copy = pltpu.make_async_copy(src, dst, isem.at[len(loads)])
        copy.start()
        loads.append(copy)
        return copy

    get_hid = load(hid, hid_v)
    get_again = load(again, again_v)

    barrier = pltpu.get_barrier_semaphore()
    ring = sorted(range(1, NZ), key=lambda d: -min(d, NZ - d))
    for k in ring:
        pl.semaphore_signal(
            barrier, inc=1, device_id=(lax.rem(y + k, NZ) * NZ + z, t), device_id_type=MESH
        )
    for k in ring:
        pl.semaphore_signal(
            barrier, inc=1, device_id=(y * NZ + lax.rem(z + k, NZ), t), device_id_type=MESH
        )
    for k in range(1, T):
        pl.semaphore_signal(barrier, inc=1, device_id=(r, lax.rem(t + k, T)), device_id_type=MESH)

    low8 = iota((8, H), 0) < 4

    def normalise(folded, gain):
        squares = jnp.sum(folded * folded, axis=1, keepdims=True)
        mean = (squares + roll4(jnp.broadcast_to(squares, (8, 128)))[:, 0:1]) * (1.0 / D)
        return folded * lax.rsqrt(mean + EPSILON) * gain

    def fold_gain(ref):
        left = jnp.broadcast_to(ref[0:H].reshape(1, H), (8, H))
        right = jnp.broadcast_to(ref[H:D].reshape(1, H), (8, H))
        return jnp.where(low8, left, right)

    get_hid.wait()
    get_again.wait()
    hidden = hid_v[...].astype(F32)
    fold_v[0:4, :] = hidden[:, 0:H]
    fold_v[4:8, :] = hidden[:, H:D]
    xg[t] = normalise(fold_v[...], fold_gain(again_v)).astype(BF)

    pl.semaphore_wait(barrier, (T - 1) + 2 * (NZ - 1))
    chip, core, chips = t // 2, lax.rem(t, 2), T // 2
    steps = sorted(range(chips), key=lambda d: (-min(d, chips - d), d))
    peers = [
        lax.rem(chip + d, chips) * 2 + (core if same else 1 - core)
        for d in steps
        for same in (1, 0)
        if d or not same
    ]

    def share(buf, phase):
        for peer in peers:
            pltpu.make_async_remote_copy(
                buf.at[t], buf.at[t], ssem.at[phase], rsem.at[phase],
                device_id=(r, peer), device_id_type=MESH,
            ).start()

    def scatter(src, dst, phase):
        for peer in peers:
            pltpu.make_async_remote_copy(
                src.at[peer], dst.at[t], ssem.at[phase], rsem.at[phase],
                device_id=(r, peer), device_id_type=MESH,
            ).start()

    offsets = sorted(
        ((dy, dz) for dy in range(NZ) for dz in range(NZ) if dy or dz),
        key=lambda d: -(min(d[0], NZ - d[0]) + min(d[1], NZ - d[1])),
    )

    def exchange(src, dst, phase):
        for dy, dz in offsets:
            peer = lax.rem(y + dy, NZ) * NZ + lax.rem(z + dz, NZ)
            pltpu.make_async_remote_copy(
                src.at[peer], dst.at[r], ssem.at[phase], rsem.at[phase],
                device_id=(peer, t), device_id_type=MESH,
            ).start()

    def arrived(buf, sems, phase):
        part = buf.at[0 : buf.shape[0] - 1]
        pltpu.make_async_copy(part, part, sems.at[phase]).wait()

    share(xg, 0)
    for k in range(1, NZ):
        pl.semaphore_signal(
            ready, inc=1, device_id=(y * NZ + lax.rem(z + k, NZ), t), device_id_type=MESH
        )
    get_ptab = load(ptab, ptab_v)
    get_ctx = load(ctx, ctx_v)
    get_mdest = load(mdest, mdest_v)
    get_wq = load(wq, wq_v.at[0 : GROUPS * HEAD_DIM])
    get_wkv = load(wkv, wkv_v)
    get_cache = load(cache, cache_v)
    get_win = load(win, win_v)
    get_wo = load(wo, wo_v.at[0 : GROUPS * HEAD_DIM])
    get_wdown = load(wdown, wdown_v)
    get_router = load(router, router_v.at[0:EXPERTS])
    get_routes = load(routes, routes_v)
    get_fgain = load(fgain, fgain_v)

    get_ptab.wait()
    get_ctx.wait()
    get_mdest.wait()
    table = ptab_v[...]
    slots = table.shape[0]
    ctx_row = ctx_v[...]
    spans = jnp.where(
        table >= 0, jnp.clip(ctx_row - iota((slots, B), 0) * PAGE, 0, PAGE), 0
    )
    tile = (iota((B, 4 * B), 0) == (iota((B, 4 * B), 1) & (B - 1))).astype(F32).astype(BF)
    table_w = mm(table.astype(F32).astype(BF), tile)
    spans_w = mm(spans.astype(F32).astype(BF), tile)
    CH = 64 if NL % 64 == 0 and NIN % 64 == 0 else 32

    def claims(base, page, head):
        found = jnp.zeros((CH, 4 * B), F32)
        pages = page.astype(F32)
        for k in range(slots):
            found = found + jnp.where(pages == table_w[k : k + 1, :], spans_w[k : k + 1, :], 0.0)
        group = iota((CH, 4 * B), 1) // B
        flag = jnp.where((group == head) & (found > 0.0), 1.0, 0.0)
        rows = jnp.where(group == GROUPS, found, flag)
        a1_v[pl.ds(base, CH), :] = jnp.where(head < GROUPS, rows, 0.0).astype(BF)

    def local_claims(c, carry):
        row = iota((CH, 4 * B), 0) + c * CH
        page = jnp.where(row < LOCAL * 8, row >> 3, -2)
        claims(pl.multiple_of(c * CH, CH), page, row & 7)
        return carry

    def inbox_claims(c, carry):
        row = iota((CH, 4 * B), 0) + c * CH
        claims(pl.multiple_of(NL + c * CH, CH), POOL + (row >> 2), row & 3)
        return carry

    lax.fori_loop(0, NL // CH, local_claims, 0)
    lax.fori_loop(0, NIN // CH, inbox_claims, 0)

    dest_row = mdest_v[...]
    dest_sq = jnp.broadcast_to(dest_row, (OUT, OUT))
    sub_sq, lane_sq = iota((OUT, OUT), 0), iota((OUT, OUT), 1)
    dest_col = jnp.sum(jnp.where(sub_sq == lane_sq, dest_sq, 0).astype(F32), axis=1, keepdims=True)
    dest_f = dest_sq.astype(F32)
    earlier = (dest_col == dest_f) & (sub_sq < lane_sq)
    rank = jnp.sum(jnp.where(earlier, 1.0, 0.0), axis=0, keepdims=True)
    slot_row = dest_f * CAP + rank
    slot_sq = slot_row[0:8, :]
    NQ = OUT * 8
    grow = (iota((OUT, NQ), 0) == (iota((OUT, NQ), 1) >> 3)).astype(F32).astype(BF)
    slot_lane = mm(slot_sq.astype(BF), grow)[0:1, :]
    pick = iota((NQ, OUT), 1) == (iota((NQ, OUT), 0) >> 3)
    slot_sub = jnp.sum(
        jnp.where(pick, jnp.broadcast_to(slot_row[0:1, :], (NQ, OUT)), 0.0), axis=1, keepdims=True
    )

    def fetch_map():
        row, lane = iota((NQ, NIN), 0), iota((NQ, NIN), 1)
        same = (lane >> 2).astype(F32) == slot_sub
        hit = same & ((row & 7) == (lane & 3)) & ((lane & 3) < GROUPS)
        return jnp.where(hit, 1.0, 0.0).astype(BF)

    def place_map():
        row, lane = iota((NIN, NQ), 0), iota((NIN, NQ), 1)
        same = (row >> 2).astype(F32) == slot_lane
        hit = same & ((lane & 7) == (row & 3)) & ((row & 3) < GROUPS)
        return jnp.where(hit, 1.0, 0.0).astype(BF)

    sq_b = iota((B, B), 0) == iota((B, B), 1)
    ctx_col = jnp.sum(
        jnp.where(sq_b, jnp.broadcast_to(ctx_row, (B, B)), 0).astype(F32), axis=1, keepdims=True
    )
    lane_b = iota((B, 128), 1)
    freq = (lane_b & 31).astype(F32)
    angle = ctx_col * jnp.exp(freq * (-2.0 * math.log(ROPE_BASE) / HEAD_DIM))
    cosine = jnp.cos(angle)
    sine = jnp.sin(angle)
    front = (lane_b & 63) < 32
    sine = jnp.where(front, -sine, sine)

    def rotate(v):
        turned = jnp.where(front, pltpu.roll(v, 96, 1), pltpu.roll(v, 32, 1))
        return (v * cosine + turned * sine).astype(BF).astype(F32)

    inq[r] = jnp.zeros((ROWS, 128), BF)
    ret[r] = jnp.zeros((ROWS, 128), BF)
    wq_v[GROUPS * HEAD_DIM :, :] = jnp.zeros((HEAD_DIM, D), BF)
    wo_v[GROUPS * HEAD_DIM :, :] = jnp.zeros((HEAD_DIM, D), BF)
    router_v[EXPERTS:, :] = jnp.zeros((128 - EXPERTS, D), BF)
    get_wq.wait()
    get_wkv.wait()

    arrived(xg, rsem, 0)
    normed = xg[...].astype(F32).reshape(T * 8, H).astype(BF)
    q_all = [mm_t(normed, wq_v[:, c * H : (c + 1) * H]) for c in range(2)]
    kv_all = [mm(normed, wkv_v[c * H : (c + 1) * H, :]) for c in range(2)]
    q01 = rotate(unfold(q_all[0][:, 0:128], q_all[1][:, 0:128], T))
    q2 = rotate(unfold(q_all[0][:, 128:256], q_all[1][:, 128:256], T))
    new_kv = unfold(kv_all[0], kv_all[1], T)
    head_lane = lane_b < 64
    heads = [
        jnp.where(head_lane, q01, 0.0),
        jnp.where(head_lane, pltpu.roll(q01, 64, 1), 0.0),
        jnp.where(head_lane, q2, 0.0),
    ]
    marker = jnp.where(head_lane, 0.0, 1.0)
    qg_v[...] = jnp.concatenate(heads + [marker], axis=0).astype(BF)

    msg[...] = mm(a1_v[NL:, :], qg_v[...]).reshape(R, ROWS, 128).astype(BF)
    pl.semaphore_wait(ready, NZ - 1)
    exchange(msg, inq, 1)

    get_cache.wait()
    key_lane = iota((8, PAGE, 128), 2) < HEAD_DIM
    for c in range(0, POOL, 8):
        values_v[c : c + 8] = jnp.where(key_lane, 1.0, cache_v[c : c + 8].astype(F32)).astype(BF)
    loc_v[0 : LOCAL * 8, :] = page_rows(
        mm(a1_v[0 : LOCAL * 8, :], qg_v[...]), cache_v[0:LOCAL], values_v[0:LOCAL]
    )
    if NL > LOCAL * 8:
        loc_v[LOCAL * 8 :, :] = jnp.zeros((NL - LOCAL * 8, 128), BF)
    eye = (iota((4 * B, 4 * B), 0) == iota((4 * B, 4 * B), 1)).astype(F32).astype(BF)
    owned_loc = mm_t(eye, a1_v[0:NL, :])[0:NR] > 0.5
    owned_in = mm_t(eye, a1_v[NL:, :])[0:NR] > 0.5
    lane_sel = iota((NR, 128), 1)
    max_sel = jnp.where((lane_sel == 0) | (lane_sel == 8) | (lane_sel == 16), 1.0, 0.0).astype(BF)
    new_key = rotate(new_kv)
    new_score = jnp.concatenate(
        [jnp.sum(h * new_key, axis=1, keepdims=True) for h in heads], axis=0
    ) * ATTN_SCALE
    fresh = jnp.where(head_lane, 1.0, new_kv.astype(BF).astype(F32))
    fresh = jnp.concatenate([fresh] * GROUPS, axis=0)
    loc = loc_v[...]
    score_loc = jnp.where(owned_loc, mm_t(max_sel, loc), NEG_FILL)
    top_loc = jnp.maximum(new_score, jnp.max(score_loc, axis=1, keepdims=True))
    sum_loc = mm(jnp.exp(score_loc - top_loc).astype(BF), loc)
    sum_loc = sum_loc + jnp.exp(new_score - top_loc) * fresh
    fetch = fetch_map()
    place = place_map()

    arrived(inq, rsem, 1)
    sent = inq[...].astype(F32).reshape(NIN, 128).astype(BF)
    lent = page_rows(mm(fetch, sent), cache_v[LOCAL:POOL], values_v[LOCAL:POOL])
    ret_s[...] = mm(place, lent).reshape(R, ROWS, 128).astype(BF)
    exchange(ret_s, ret, 2)

    get_win.wait()
    win_f[...] = win_v[...].astype(F32)
    wgu_v[:, 0:UNITS] = win_f[pl.ds(0, D, stride=2), :].astype(BF)
    wgu_v[:, UNITS:] = win_f[pl.ds(1, D, stride=2), :].astype(BF)
    get_wo.wait()
    get_wdown.wait()
    get_router.wait()
    get_routes.wait()
    get_fgain.wait()
    eye_b = sq_b.astype(F32).astype(BF)
    chosen = mm_t(eye_b, routes_v[...].astype(F32).astype(BF))
    expert = iota((B, 128), 1)
    expert_f = expert.astype(F32)
    picked = jnp.zeros((B, 128), F32)
    for k in range(routes.shape[0]):
        picked = jnp.where(expert_f == chosen[:, k : k + 1], 1.0, picked)
    mine = expert == (t * UNITS) // FF
    gain_f = fold_gain(fgain_v)
    residual = fold_v[...]

    arrived(ret, rsem, 2)
    back = ret[...].astype(F32).reshape(NIN, 128).astype(BF)
    score_in = jnp.where(owned_in, mm_t(max_sel, back), NEG_FILL)
    top = jnp.maximum(top_loc, jnp.max(score_in, axis=1, keepdims=True))
    merged = jnp.exp(top_loc - top) * sum_loc + mm(jnp.exp(score_in - top).astype(BF), back)
    attention = (merged / merged[:, 32:33]).astype(BF).astype(F32)
    att0, att1, att2 = (attention[g * B : (g + 1) * B] for g in range(GROUPS))
    left = jnp.where(head_lane, pltpu.roll(att0, 64, 1), att1)
    right = jnp.where(head_lane, pltpu.roll(att2, 64, 1), 0.0)
    left1, left2 = expand(left, T)
    right1, right2 = expand(right, T)
    rows1 = jnp.concatenate([left1, right1], axis=1)
    rows2 = jnp.concatenate([left2, right2], axis=1)
    partial = mm(rows1, wo_v[:, 0:H]) + mm(rows2, wo_v[:, H:D])
    partial = partial.reshape(T, 8, H).astype(BF)
    rs_s[...] = partial
    scatter(rs_s, rs, 3)
    rs[t] = rs_s[t]
    arrived(rs, rsem, 3)
    summed = jnp.sum(rs[...].astype(F32), axis=0)
    attended = (residual + RESID_SCALE * summed).astype(BF)
    attended_f = attended.astype(F32)
    fg[t] = normalise(attended_f, gain_f).astype(BF)
    share(fg, 4)
    both_o[:, 0:H] = attended_f[0:4].astype(BF)
    both_o[:, H:D] = attended_f[4:8].astype(BF)

    arrived(fg, rsem, 4)
    ffn = fg[...].astype(F32).reshape(T * 8, H).astype(BF)
    up_all = [mm(ffn, wgu_v[c * H : (c + 1) * H, :]) for c in range(2)]
    log_all = [mm_t(ffn, router_v[:, c * H : (c + 1) * H]) for c in range(2)]
    gate = unfold(up_all[0][:, 0:UNITS], up_all[1][:, 0:UNITS], T)
    up = unfold(up_all[0][:, UNITS:], up_all[1][:, UNITS:], T)
    logits = jnp.where(picked > 0.0, unfold(log_all[0], log_all[1], T), NEG_FILL)
    chances = jnp.exp(logits - jnp.max(logits, axis=1, keepdims=True))
    chances = jnp.where(picked > 0.0, chances, 0.0)
    share_of = jnp.sum(jnp.where(mine, chances, 0.0), axis=1, keepdims=True) / jnp.sum(
        chances, axis=1, keepdims=True
    )
    active = gate * (1.0 / (1.0 + jnp.exp(-gate))) * up * share_of
    act1, act2 = expand(active, T)
    down = mm(act1, wdown_v[:, 0:H]) + mm(act2, wdown_v[:, H:D])
    es_s[...] = down.reshape(T, 8, H).astype(BF)
    scatter(es_s, es, 5)
    es[t] = es_s[t]
    arrived(es, rsem, 5)
    experts = jnp.sum(es[...].astype(F32), axis=0)
    both_o[:, D : D + H] = experts[0:4].astype(BF)
    both_o[:, D + H :] = experts[4:8].astype(BF)
    for phase, buf in enumerate((xg, inq, ret, rs, fg, es)):
        arrived(buf, ssem, phase)


def on_device(
    hidden,
    attn_gain,
    w_query,
    w_keyvalue,
    w_output,
    cache,
    page_table,
    ctx_len,
    move_dest,
    ffn_gain,
    router,
    routes,
    w_in,
    w_down,
):
    R = lax.axis_size("replica")
    T = lax.axis_size("tensor")
    D = hidden.shape[1]
    H = D // 2
    B = page_table.shape[0]
    POOL = cache.shape[0]
    OUT = move_dest.shape[0]
    LOCAL = POOL - OUT
    UNITS = w_down.shape[0]
    NL = -(-LOCAL * 8 // 128) * 128
    NIN = R * ROWS
    args = (
        hidden,
        attn_gain,
        w_query.T,
        w_keyvalue.reshape(D, 2 * HEAD_DIM),
        w_output,
        cache.reshape(POOL, PAGE, 2 * HEAD_DIM),
        page_table.T,
        ctx_len.reshape(1, B),
        move_dest.reshape(1, OUT),
        ffn_gain,
        router.T,
        routes.T,
        w_in.reshape(2 * D, UNITS),
        w_down,
    )
    vm = pltpu.VMEM
    landing = [vm(a.shape, a.dtype) for a in args]
    landing[2] = vm((256, D), BF)
    landing[4] = vm((256, D), BF)
    landing[10] = vm((128, D), BF)
    any_spec = pl.BlockSpec(memory_space=pltpu.HBM)
    group = vm((T, 8, H), BF)
    inbox = vm((R, ROWS, 128), BF)
    scratch = landing + [
        vm((2 * D, UNITS), F32),
        vm((D, 2 * UNITS), BF),
        vm((8, H), F32),
        vm((NL + NIN, 4 * B), BF),
        vm((4 * B, 128), BF),
        vm((NL, 128), BF),
        vm((POOL, PAGE, 128), BF),
        group,
        inbox,
        inbox,
        inbox,
        inbox,
        group,
        group,
        group,
        group,
        group,
        pltpu.SemaphoreType.DMA((len(args),)),
        pltpu.SemaphoreType.REGULAR,
        pltpu.SemaphoreType.DMA((6,)),
        pltpu.SemaphoreType.DMA((6,)),
    ]
    both = pl.pallas_call(
        functools.partial(kernel, R, T, B, NL, LOCAL, POOL, OUT, UNITS),
        out_shape=pltpu.VMEM((4, 2 * D), BF),
        in_specs=[any_spec] * len(args),
        out_specs=pl.BlockSpec(memory_space=pltpu.VMEM),
        scratch_shapes=scratch,
        name="decode_step",
        compiler_params=pltpu.CompilerParams(
            collective_id=0, has_side_effects=True, vmem_limit_bytes=32 * 1024 * 1024
        ),
    )(*[pltpu.with_memory_space_constraint(a, pltpu.HBM) for a in args])
    return both[:, 0:D], both[:, D:]


def solution(mesh):
    placed = (
        P(("replica", "tensor"), None),
        P(),
        P(None, "tensor"),
        P(None, "tensor", None),
        P("tensor", None),
        P("replica", None, "tensor", None),
        P("replica", None),
        P("replica"),
        P("replica"),
        P(),
        P(),
        P("replica", None),
        P(None, None, "tensor"),
        P("tensor", None),
    )
    return jax.shard_map(
        on_device,
        mesh=mesh,
        in_specs=placed,
        out_specs=(P(("replica", "tensor"), None), P(("replica", "tensor"), None)),
        check_vma=False,
    )
```
